32 devices in a mesh: wide: 8 (over z, x), narrow: 4 (over y, core).
Axes of the slice: x: 2, y: 2, z: 4, core: 2. Of those that a mesh axis runs over, the one named last changes fastest.
Arguments:
- tokens: bfloat16 [8, 1024, 1120], P('wide', 'narrow'), may hold values from -6 to 6
- lengths: int32 [8], P('wide'), may hold values from 128 to 1024, as said below
- norm_one: float32 [1120], replicated, may hold values from 0.25 to 1.75
- qkv_weight: bfloat16 [3, 1120, 1120], P(None, None, 'narrow'), may hold values from -0.25 to 0.25
- out_weight: bfloat16 [1120, 1120], P('narrow'), may hold values from -3 to 3
- norm_two: float32 [1120], replicated, may hold values from 0.25 to 1.75
- up_weight: bfloat16 [1120, 4480], P(None, 'narrow'), may hold values from -0.1875 to 0.1875
- down_weight: bfloat16 [4480, 1120], P('narrow'), may hold values from -0.09375 to 0.09375
- grad_out: bfloat16 [8, 1024, 1120], P('wide', 'narrow'), may hold values from -6 to 6
Outputs:
- block_output: bfloat16 [8, 1024, 1120], P('wide', 'narrow')
- input_grad: bfloat16 [8, 1024, 1120], P('wide', 'narrow')
- norm_one_grad: float32 [1120], replicated
- qkv_grad: float32 [3, 1120, 1120], P(None, None, 'narrow')
- out_grad: float32 [1120, 1120], P('narrow')
- norm_two_grad: float32 [1120], replicated
- up_grad: float32 [1120, 4480], P(None, 'narrow')
- down_grad: float32 [4480, 1120], P('narrow')
The draws below stay inside these ranges and needn't reach their ends.
Inputs may be any that keep to these rules, and one draw needn't show every extreme that they name: `lengths`: each cell's count of real genes; some cell has exactly 1024 and some other exactly 128.
All inputs are finite; a program needn't handle non-finite values.
Results may differ from the reference program's by a relative error of at most 0.013.
The reference program's roundings to bfloat16 on the way count: a program that leaves them out, or rounds other values in their place, can miss the bound.
Values may be sent and summed in bfloat16 or wider, within the bound.
No kernel may reach another device: no remote copies, remote signals or barrier semaphores. Data moves between devices by JAX's collectives and lax.ppermute only.
A program may use at most 192 MiB of HBM per device.

```python
import jax
import jax.numpy as jnp
from jax import lax

D = 1120
HEADS = 20
HS = 56
FF = 4480
LEN = 1024
MINLEN = 128
CELLS = 8


def draw_lengths(key, part):
    first_key = jax.random.fold_in(key, 11)
    second_key = jax.random.fold_in(key, 12)
    third_key = jax.random.fold_in(key, 13)
    spread = jax.random.randint(first_key, (CELLS,), 0, 1024)
    lengths = LEN - (LEN - MINLEN) * (spread * spread // 1024) // 1024
    longest = jax.random.randint(second_key, (), 0, CELLS)
    shortest = (longest + 1 + jax.random.randint(third_key, (), 0, CELLS - 1)) % CELLS
    places = jnp.arange(CELLS)
    lengths = jnp.where(places == longest, LEN, jnp.where(places == shortest, MINLEN, lengths))
    return lengths.astype(jnp.int32)


def block_scale(stream_key, shape, cuts, least, top_value):
    def one(axis_at, parts):
        steps = jax.random.uniform(jax.random.fold_in(jax.random.fold_in(stream_key, 6), axis_at), (parts,), jnp.float32, least / len(cuts), top_value / len(cuts))
        return jnp.repeat(jnp.exp(steps), shape[axis_at] // parts).reshape((-1,) + (1,) * (len(shape) - axis_at - 1))

    level = one(*cuts[0])
    for cut in cuts[1:]:
        level = level * one(*cut)
    return level


def gaussian(own_key, dims, deviation, bound, pieces=(), dtype=jnp.bfloat16):
    drawn = jax.random.normal(own_key, dims, jnp.float32) * deviation
    if len(pieces) > 0:
        drawn = block_scale(own_key, dims, pieces, -0.22, 0.18) * drawn
    return jnp.clip(drawn, min=-bound, max=bound).astype(dtype)


def setup_inputs(seed: int = 0) -> dict:
    key_of = jax.random.split(jax.random.key(seed), 10)
    tokens = gaussian(key_of[0], (CELLS, LEN, D), 1.0, 6.0, ((0, 8), (1, 4)))
    lengths = draw_lengths(jax.random.fold_in(key_of[9], 71), 0)
    norm_one = jnp.clip(1.0 + 0.15 * jax.random.normal(key_of[2], (D,), jnp.float32), 0.25, 1.75)
    qkv_weight = gaussian(key_of[3], (3, D, D), (D // 2) ** -0.5, 0.25, ((2, 4),))
    out_weight = gaussian(key_of[4], (D, D), (max(4 * D // LEN, 1)) ** -0.5, 3.0, ((0, 4),))
    norm_two = jnp.clip(1.0 + 0.15 * jax.random.normal(key_of[5], (D,), jnp.float32), 0.25, 1.75)
    up_weight = gaussian(key_of[6], (D, FF), D ** -0.5, 0.1875, ((1, 4),))
    down_weight = gaussian(key_of[7], (FF, D), FF ** -0.5, 0.09375, ((0, 4),))
    grad_out = gaussian(key_of[8], (CELLS, LEN, D), 1.0, 6.0, ((0, 8), (1, 4)))
    return dict(tokens=tokens, lengths=lengths, norm_one=norm_one, qkv_weight=qkv_weight, out_weight=out_weight, norm_two=norm_two, up_weight=up_weight, down_weight=down_weight, grad_out=grad_out)


@jax.custom_vjp
def low(v):
    return lax.optimization_barrier(v.astype(jnp.bfloat16)).astype(jnp.float32)

@jax.custom_vjp
def low_back(v):
    return v

def low_keep(v):
    return (low(v), None)

def low_pass(kept, grad):
    return (grad,)

def back_keep(v):
    return (v, None)

def back_low(kept, grad):
    return (low(grad),)
low.defvjp(low_keep, low_pass)
low_back.defvjp(back_keep, back_low)

def normalize(values):
    center = values - lax.optimization_barrier(jnp.mean(values, axis=-1, keepdims=True))
    spread = lax.optimization_barrier(jnp.mean(center * center, axis=-1, keepdims=True))
    return center * lax.rsqrt(spread + 1e-05)

def key_mask(positions, length):
    rows_index = lax.broadcasted_iota(jnp.int32, (positions, positions), 0)
    cols_index = lax.broadcasted_iota(jnp.int32, (positions, positions), 1)
    return (cols_index <= rows_index) & (cols_index < length)

def cell_forward(weights, cell_tokens, length):
    norm_one, qkv_weight, out_weight, norm_two, up_weight, down_weight = weights
    highest = lax.Precision.HIGHEST
    positions = cell_tokens.shape[0]
    live_rows = (lax.broadcasted_iota(jnp.int32, (positions, 1), 0) < length).astype(jnp.float32)
    normed = low(normalize(cell_tokens) * norm_one)
    projected = low(low_back(jnp.einsum('ld,tde->tle', normed, qkv_weight, precision=highest)))
    head_split = projected.reshape(3, positions, HEADS, HS)
    raw_scores = jnp.einsum('qhe,khe->hqk', head_split[0], head_split[1], precision=highest) * HS ** (-0.5)
    scores = jnp.where(key_mask(positions, length)[None], low_back(raw_scores), -1e+30)
    top_score = lax.optimization_barrier(jnp.max(scores, axis=-1, keepdims=True))
    exp_scores = jnp.exp(scores - top_score)
    attn_probs = low(exp_scores / lax.optimization_barrier(jnp.sum(exp_scores, axis=-1, keepdims=True)))
    mixed_heads = jnp.einsum('hqk,khe->qhe', attn_probs, head_split[2], precision=highest)
    mixed_heads = low(low_back(mixed_heads.reshape(positions, HEADS * HS)))
    branch = low_back(jnp.dot(mixed_heads, out_weight, precision=highest))
    middle = cell_tokens + live_rows * branch
    normed_two = low(normalize(middle) * norm_two)
    pre_act = low_back(jnp.dot(normed_two, up_weight, precision=highest))
    hidden = low(jax.nn.gelu(pre_act, approximate=False))
    branch_two = low_back(jnp.dot(hidden, down_weight, precision=highest))
    return middle + live_rows * branch_two

def reference(tokens, lengths, norm_one, qkv_weight, out_weight, norm_two, up_weight, down_weight, grad_out):

    def whole_block(cells_in, gain_one, proj_qkv, proj_out, gain_two, proj_up, proj_down):
        weights = (gain_one, proj_qkv, proj_out, gain_two, proj_up, proj_down)

        def one_cell(cell_item):
            return cell_forward(weights, cell_item[0], cell_item[1])
        return lax.map(jax.checkpoint(one_cell), (cells_in, lengths))
    outputs, pull_back = jax.vjp(whole_block, tokens.astype(jnp.float32), norm_one.astype(jnp.float32), qkv_weight.astype(jnp.float32), out_weight.astype(jnp.float32), norm_two.astype(jnp.float32), up_weight.astype(jnp.float32), down_weight.astype(jnp.float32))
    gradients = pull_back(grad_out.astype(jnp.float32))
    return (outputs.astype(jnp.bfloat16), gradients[0].astype(jnp.bfloat16), gradients[1], gradients[2], gradients[3], gradients[4], gradients[5], gradients[6])
```

```python
import jax
import jax.numpy as jnp
from jax import lax
from jax.sharding import PartitionSpec as P

HS = 56
HP = 64
F32 = jnp.float32
BF16 = jnp.bfloat16


def layer_stats(values):
    mean = jnp.mean(values, axis=-1, keepdims=True)
    center = values - mean
    spread = jnp.mean(center * center, axis=-1, keepdims=True)
    rstd = lax.rsqrt(spread + 1e-05)
    return center * rstd, rstd


def layer_back(grad_scaled, normal, rstd):
    first = jnp.mean(grad_scaled, axis=-1, keepdims=True)
    second = jnp.mean(grad_scaled * normal, axis=-1, keepdims=True)
    return rstd * (grad_scaled - first - normal * second)


def dot(a, b, dims):
    return lax.dot_general(a, b, (dims, ((), ())), preferred_element_type=F32)


class Narrow:
    def __init__(self, size):
        self.perm = {k: [(i, i ^ k) for i in range(size)] for k in (1, 2, 3)}

    def send(self, value, k):
        return lax.ppermute(value, "narrow", self.perm[k])

    def gather(self, value):
        across = self.send(value, 2)
        return [value, self.send(value, 1), across, self.send(across, 1)]

    def exchange(self, blocks):
        return [blocks[0]] + [self.send(blocks[k], k) for k in (1, 2, 3)]

    def scatter_sum(self, terms, rows):
        part = [terms[k * rows : (k + 1) * rows] for k in range(4)]
        got = self.send(
            jnp.concatenate([part[1].astype(BF16), part[3].astype(BF16)], axis=0), 1
        ).astype(F32)
        far = (part[2] + got[rows:]).astype(BF16)
        return part[0] + got[:rows] + self.send(far, 2).astype(F32)


class Ring:
    def __init__(self, size):
        order = list(range(0, size, 2)) + list(range(size - 1, 0, -2))
        self.size = size
        pairs = [(order[i], order[(i + 1) % size]) for i in range(size)]
        self.perm = {1: pairs, -1: [(b, a) for a, b in pairs]}
        index = lax.axis_index("wide")
        self.place = jnp.where(index % 2 == 0, index // 2, size - 1 - index // 2)

    def pick(self, chunks, at):
        return lax.dynamic_index_in_dim(chunks, jnp.mod(at, self.size), 0, keepdims=False)

    def reduce(self, chunks, way):
        current = self.pick(chunks, self.place - way)
        for step in range(self.size - 1):
            got = lax.ppermute(current, "wide", self.perm[way])
            mine = self.pick(chunks, self.place - way * (2 + step))
            current = (got.astype(F32) + mine.astype(F32)).astype(BF16)
        return current

    def spread(self, current, way):
        whole = jnp.zeros((self.size,) + current.shape, F32)
        for step in range(self.size):
            at = jnp.mod(self.place - way * step, self.size)
            whole = lax.dynamic_update_index_in_dim(whole, current.astype(F32), at, 0)
            if step < self.size - 1:
                current = lax.ppermute(current, "wide", self.perm[way])
        return whole

    def total(self, chunks, way):
        if self.size > 8:
            return lax.psum(chunks.astype(F32), "wide")
        return self.spread(self.reduce(chunks, way), way)


def head_split(values):
    rows = values.shape[0]
    return values.reshape(rows, -1, HP)


def masked_scores(queries, keys_in, allowed):
    scores = jnp.einsum("qhe,khe->hqk", queries, keys_in, preferred_element_type=F32) * HS ** (-0.5)
    return jnp.where(allowed[None], scores, -1e30)


def attend(queries, keys_in, values_in, allowed):
    scores = masked_scores(queries, keys_in, allowed)
    top = jnp.max(scores, axis=-1, keepdims=True)
    exp_scores = jnp.exp(scores - top)
    total = jnp.sum(exp_scores, axis=-1, keepdims=True)
    probs = (exp_scores / total).astype(BF16)
    mixed = jnp.einsum("hqk,khe->qhe", probs, values_in, preferred_element_type=F32)
    return mixed.astype(BF16), top + jnp.log(total)


def attend_back(queries, keys_in, values_in, log_total, grad_mixed, allowed):
    scores = masked_scores(queries, keys_in, allowed)
    probs = jnp.exp(scores - log_total)
    grad_values = jnp.einsum("hqk,qhe->khe", probs.astype(BF16), grad_mixed, preferred_element_type=F32)
    grad_probs = jnp.einsum("qhe,khe->hqk", grad_mixed, values_in, preferred_element_type=F32)
    inner = jnp.sum(probs * grad_probs, axis=-1, keepdims=True)
    grad_scores = (probs * (grad_probs - inner)).astype(BF16)
    grad_queries = jnp.einsum("hqk,khe->qhe", grad_scores, keys_in, preferred_element_type=F32) * HS ** (-0.5)
    grad_keys = jnp.einsum("hqk,qhe->khe", grad_scores, queries, preferred_element_type=F32) * HS ** (-0.5)
    return [g.astype(BF16) for g in (grad_queries, grad_keys, grad_values)]


def make(sizes):
    wide, parts = sizes["wide"], sizes["narrow"]

    def on_device(
        tokens, lengths, norm_one, qkv_weight, out_weight, norm_two, up_weight, down_weight, grad_out
    ):
        cell_count, rows, width = tokens.shape
        own_width = qkv_weight.shape[2]
        heads = own_width // HS
        pad_heads = heads + heads % 2
        pad_width = pad_heads * HP
        units = up_weight.shape[1]
        chunk = -(-max(width, units) // (wide * 16)) * 16
        tall = chunk * wide
        narrow, ring = Narrow(parts), Ring(wide)
        me = lax.axis_index("narrow")
        length = lengths[0]
        own_tokens, own_grad = tokens[0], grad_out[0]
        block_index = jnp.bitwise_xor(me, jnp.arange(parts, dtype=jnp.int32))
        positions = (block_index[:, None] * rows + jnp.arange(rows, dtype=jnp.int32)[None]).reshape(-1)
        own_live = (me * rows + lax.broadcasted_iota(jnp.int32, (rows, 1), 0) < length).astype(F32)

        token_blocks = narrow.gather(own_tokens)
        own_branch = (own_live * own_grad.astype(F32)).astype(BF16)
        out_own, own_branch, token_blocks = lax.optimization_barrier((out_weight, own_branch, token_blocks))
        out_blocks = narrow.gather(out_own)
        grad_blocks = narrow.gather(own_branch)

        def pad_cols(weight):
            split = weight.reshape(width, heads, HS)
            return jnp.pad(split, ((0, 0), (0, pad_heads - heads), (0, HP - HS))).reshape(width, pad_width)

        def pad_rows(weight):
            split = weight.reshape(heads, HS, width)
            return jnp.pad(split, ((0, pad_heads - heads), (0, HP - HS), (0, 0))).reshape(pad_width, width)

        proj = jnp.concatenate([pad_cols(qkv_weight[t]) for t in range(3)], axis=1)
        stream = own_tokens.astype(F32)
        normal_one, rstd_one = layer_stats(stream)
        rows_one = jnp.concatenate(
            [(layer_stats(b.astype(F32))[0] * norm_one).astype(BF16) for b in token_blocks], axis=0
        )
        projected = dot(rows_one, proj, ((1,), (0,))).astype(BF16)
        queries, keys_in, values_in = (
            head_split(projected[:, t * pad_width : (t + 1) * pad_width]) for t in range(3)
        )
        allowed = (positions[None, :] <= positions[:, None]) & (positions[None, :] < length)
        mixed, log_total = attend(queries, keys_in, values_in, allowed)
        mixed = mixed.reshape(-1, pad_width)
        mixed_parts = narrow.exchange([mixed[k * rows : (k + 1) * rows] for k in range(4)])
        mixed_own = jnp.concatenate(mixed_parts, axis=1)
        out_all = jnp.concatenate([pad_rows(b) for b in out_blocks], axis=0)
        middle = stream + own_live * dot(mixed_own, out_all, ((1,), (0,)))
        normal_two, rstd_two = layer_stats(middle)
        rows_two = jnp.concatenate(narrow.gather((normal_two * norm_two).astype(BF16)), axis=0)
        grad_rows = jnp.concatenate(grad_blocks, axis=0)
        pre_act = dot(rows_two, up_weight, ((1,), (0,)))
        grad_hidden = dot(grad_rows, down_weight, ((1,), (1,)))
        cdf = 0.5 * (1.0 + lax.erf(pre_act * 0.5**0.5))
        slope = cdf + pre_act * jnp.exp(-0.5 * pre_act * pre_act) * (0.5 / jnp.pi) ** 0.5
        hidden = (pre_act * cdf).astype(BF16)
        grad_pre = (grad_hidden * slope).astype(BF16)

        def ring_form(left, right):
            left = jnp.pad(left, ((0, 0), (0, tall - left.shape[1])))
            return dot(left, right, ((0,), (0,))).astype(BF16).reshape(wide, chunk, right.shape[1])

        down_sum = ring.total(ring_form(hidden, grad_rows), 1)
        up_sum = ring.total(ring_form(rows_two, grad_pre), -1)
        terms_two = dot(grad_pre, up_weight, ((1,), (1,)))
        grad_normed_two = narrow.scatter_sum(terms_two, rows)
        mlp_terms = dot(hidden, down_weight, ((1,), (0,)))
        mlp_own = narrow.scatter_sum(mlp_terms, rows)
        block_output = (middle + own_live * mlp_own).astype(BF16)

        gain_two = jnp.sum(grad_normed_two * normal_two, axis=0)
        grad_middle = own_grad.astype(F32) + layer_back(grad_normed_two * norm_two, normal_two, rstd_two)
        grad_attn = (own_live * grad_middle).astype(BF16)
        grad_all = dot(grad_attn, out_all, ((1,), (1,))).astype(BF16)
        grad_mixed = jnp.concatenate(
            narrow.exchange([grad_all[:, k * pad_width : (k + 1) * pad_width] for k in range(4)]), axis=0
        )
        attn_rows = jnp.concatenate(narrow.gather(grad_attn), axis=0)
        grad_parts = attend_back(queries, keys_in, values_in, log_total, head_split(grad_mixed), allowed)
        grad_proj = jnp.concatenate([g.reshape(-1, pad_width) for g in grad_parts], axis=1)
        terms_one = dot(grad_proj, proj, ((1,), (1,)))
        grad_normed_one = narrow.scatter_sum(terms_one, rows)
        gain_one = jnp.sum(grad_normed_one * normal_one, axis=0)
        grad_stream = layer_back(grad_normed_one * norm_one, normal_one, rstd_one)
        input_grad = (grad_middle + grad_stream).astype(BF16)

        live_width = heads * HP
        left = jnp.concatenate(
            [grad_proj[:, t * pad_width : t * pad_width + live_width] for t in range(3)], axis=1
        )
        last = jnp.concatenate(
            [
                dot(left, rows_one, ((0,), (0,))).astype(BF16),
                dot(mixed[:, :live_width], attn_rows, ((0,), (0,))).astype(BF16),
            ],
            axis=0,
        )
        tail = -(-last.shape[0] // (wide * 16)) * 16
        last = jnp.pad(last, ((0, tail * wide - last.shape[0]), (0, 0))).reshape(wide, tail, width)
        half = tail // 2
        last_sum = jnp.concatenate(
            [ring.total(last[:, :half], 1), ring.total(last[:, half:], -1)], axis=1
        ).reshape(tail * wide, width)

        gains = jnp.stack([gain_one, gain_two])
        for k in (1, 2):
            gains = gains + narrow.send(gains, k)
        hop = 1
        while hop < wide:
            gains = gains + lax.ppermute(gains, "wide", [(i, i ^ hop) for i in range(wide)])
            hop *= 2

        split = last_sum[: 4 * live_width].reshape(4, heads, HP, width)[:, :, :HS]
        qkv_grad = split[:3].reshape(3, own_width, width).transpose(0, 2, 1)
        out_grad = split[3].reshape(own_width, width)
        down_grad = down_sum.reshape(tall, width)[:units]
        up_grad = up_sum.reshape(tall, units)[:width]
        return (
            block_output[None],
            input_grad[None],
            gains[0],
            qkv_grad,
            out_grad,
            gains[1],
            up_grad,
            down_grad,
        )

    return on_device


def solution(mesh):
    in_specs = (
        P("wide", "narrow", None),
        P("wide"),
        P(),
        P(None, None, "narrow"),
        P("narrow", None),
        P(),
        P(None, "narrow"),
        P("narrow", None),
        P("wide", "narrow", None),
    )
    out_specs = (
        P("wide", "narrow", None),
        P("wide", "narrow", None),
        P(),
        P(None, None, "narrow"),
        P("narrow", None),
        P(),
        P(None, "narrow"),
        P("narrow", None),
    )
    return jax.shard_map(
        make(dict(mesh.shape)), mesh=mesh, in_specs=in_specs, out_specs=out_specs, check_vma=False
    )
```

```python
from functools import partial

import jax
import jax.numpy as jnp
from jax import lax
from jax.experimental import pallas as pl
from jax.experimental.pallas import tpu as pltpu
from jax.sharding import PartitionSpec as P

HS = 56
HP = 64
F32 = jnp.float32
BF16 = jnp.bfloat16


def layer_stats(values):
    mean = jnp.mean(values, axis=-1, keepdims=True)
    center = values - mean
    spread = jnp.mean(center * center, axis=-1, keepdims=True)
    rstd = lax.rsqrt(spread + 1e-05)
    return center * rstd, rstd


def layer_back(grad_scaled, normal, rstd):
    first = jnp.mean(grad_scaled, axis=-1, keepdims=True)
    second = jnp.mean(grad_scaled * normal, axis=-1, keepdims=True)
    return rstd * (grad_scaled - first - normal * second)


def dot(a, b, dims):
    return lax.dot_general(a, b, (dims, ((), ())), preferred_element_type=F32)


class Narrow:
    def __init__(self, size):
        self.perm = {k: [(i, i ^ k) for i in range(size)] for k in (1, 2, 3)}

    def send(self, value, k):
        return lax.ppermute(value, "narrow", self.perm[k])

    def gather(self, value):
        across = self.send(value, 2)
        return [value, self.send(value, 1), across, self.send(across, 1)]

    def exchange(self, blocks):
        return [blocks[0]] + [self.send(blocks[k], k) for k in (1, 2, 3)]

    def scatter_sum(self, terms, rows):
        part = [terms[k * rows : (k + 1) * rows] for k in range(4)]
        got = self.send(
            jnp.concatenate([part[1].astype(BF16), part[3].astype(BF16)], axis=0), 1
        ).astype(F32)
        far = (part[2] + got[rows:]).astype(BF16)
        return part[0] + got[:rows] + self.send(far, 2).astype(F32)


class Ring:
    def __init__(self, size):
        order = list(range(0, size, 2)) + list(range(size - 1, 0, -2))
        self.size = size
        pairs = [(order[i], order[(i + 1) % size]) for i in range(size)]
        self.perm = {1: pairs, -1: [(b, a) for a, b in pairs]}
        index = lax.axis_index("wide")
        self.place = jnp.where(index % 2 == 0, index // 2, size - 1 - index // 2)

    def pick(self, chunks, at):
        return lax.dynamic_index_in_dim(chunks, jnp.mod(at, self.size), 0, keepdims=False)

    def reduce(self, chunks, way):
        current = self.pick(chunks, self.place - way)
        for step in range(self.size - 1):
            got = lax.ppermute(current, "wide", self.perm[way])
            mine = self.pick(chunks, self.place - way * (2 + step))
            current = (got.astype(F32) + mine.astype(F32)).astype(BF16)
        return current

    def spread(self, current, way):
        whole = jnp.zeros((self.size,) + current.shape, F32)
        for step in range(self.size):
            at = jnp.mod(self.place - way * step, self.size)
            whole = lax.dynamic_update_index_in_dim(whole, current.astype(F32), at, 0)
            if step < self.size - 1:
                current = lax.ppermute(current, "wide", self.perm[way])
        return whole

    def total(self, chunks, way):
        if self.size > 8:
            return lax.psum(chunks.astype(F32), "wide")
        return self.spread(self.reduce(chunks, way), way)


LOG2E = 1.4426950408889634
SCALE = HS**-0.5


def nt(a, b):
    return lax.dot_general(a, b, (((1,), (1,)), ((), ())), preferred_element_type=F32)


def nn(a, b):
    return lax.dot_general(a, b, (((1,), (0,)), ((), ())), preferred_element_type=F32)


def half_of(values, which):
    lane = lax.broadcasted_iota(jnp.int32, values.shape, 1)
    keep = lane < HP if which == 0 else lane >= HP
    return jnp.where(keep, values, jnp.zeros_like(values))


def causal_tile(rows):
    key = lax.broadcasted_iota(jnp.int32, (rows, rows), 0)
    query = lax.broadcasted_iota(jnp.int32, (rows, rows), 1)
    return key <= query


def for_pair(body, last_heads):
    last = pl.num_programs(0) - 1

    @pl.when(pl.program_id(0) < last)
    def _():
        body(2)

    @pl.when(pl.program_id(0) == last)
    def _():
        body(last_heads)


def attend_kernel(last_heads, me_ref, *refs):
    q, k, v, (o_ref, lse_ref) = refs[0:4], refs[4:8], refs[8:12], refs[12:14]
    me = me_ref[0]
    rows = q[0].shape[0]

    def body(heads):
        value_t = [v[j][...].T for j in range(4)]
        causal = causal_tile(rows)
        for a in range(4):
            outs = []
            for h in range(heads):
                query = half_of(q[a][...], h)
                score = [nt(k[j][...], query) for j in range(a + 1)]
                score[a] = jnp.where(causal, score[a], -1e30)
                top = jnp.max(score[0], axis=0, keepdims=True)
                for j in range(1, a + 1):
                    top = jnp.maximum(top, jnp.max(score[j], axis=0, keepdims=True))
                top = top * (SCALE * LOG2E)
                total = jnp.zeros((1, rows), F32)
                acc = jnp.zeros((HP, rows), F32)
                for j in range(a + 1):
                    p = jnp.exp2(score[j] * (SCALE * LOG2E) - top)
                    total = total + jnp.sum(p, axis=0, keepdims=True)
                    acc = acc + nn(value_t[j][h * HP : (h + 1) * HP], p.astype(BF16))
                outs.append(acc / total)
                lse_ref[0, a, h : h + 1, :] = top + jnp.log2(total)
            if heads == 1:
                outs.append(jnp.zeros((HP, rows), F32))
            at = pl.multiple_of(jnp.bitwise_xor(me, a) * rows, rows)
            o_ref[pl.ds(at, rows), :] = jnp.concatenate(outs, axis=0).T.astype(BF16)

    for_pair(body, last_heads)


def attend_back_kernel(last_heads, me_ref, *refs):
    q, k, v, do, o = (refs[4 * i : 4 * i + 4] for i in range(5))
    lse_ref, g_ref, dk_acc, dv_acc = refs[20:24]
    me = me_ref[0]
    rows = q[0].shape[0]

    def body(heads):
        key_t = [k[j][...].T for j in range(4)]
        causal = causal_tile(rows)
        for a in range(4):
            grad = do[a][...]
            product = (grad.astype(F32) * o[a][...].astype(F32)).T
            grads_q = []
            for h in range(heads):
                query, grad_h = half_of(q[a][...], h), half_of(grad, h)
                inner = jnp.sum(product[h * HP : (h + 1) * HP], axis=0, keepdims=True)
                lse = lse_ref[0, a, h : h + 1, :]
                dq = jnp.zeros((HP, rows), F32)
                for j in range(a + 1):
                    score = nt(k[j][...], query) * (SCALE * LOG2E) - lse
                    if j == a:
                        score = jnp.where(causal, score, -1e30)
                    p = jnp.exp2(score)
                    ds = (p * (nt(v[j][...], grad_h) - inner)).astype(BF16)
                    dv, dk = nn(p.astype(BF16), grad_h), nn(ds, query)
                    if a == j and h == 0:
                        dv_acc[j], dk_acc[j] = dv, dk
                    else:
                        dv_acc[j] = dv_acc[j] + dv
                        dk_acc[j] = dk_acc[j] + dk
                    dq = dq + nn(key_t[j][h * HP : (h + 1) * HP], ds)
                grads_q.append(dq * SCALE)
            if heads == 1:
                grads_q.append(jnp.zeros((HP, rows), F32))
            at = pl.multiple_of(jnp.bitwise_xor(me, a) * rows, rows)
            g_ref[0, pl.ds(at, rows), :] = jnp.concatenate(grads_q, axis=0).T.astype(BF16)
        for j in range(4):
            at = pl.multiple_of(jnp.bitwise_xor(me, j) * rows, rows)
            g_ref[1, pl.ds(at, rows), :] = (dk_acc[j] * SCALE).astype(BF16)
            g_ref[2, pl.ds(at, rows), :] = dv_acc[j].astype(BF16)

    for_pair(body, last_heads)


def block_specs(rows, pairs, t):
    return [
        pl.BlockSpec((rows, 128), lambda p, m, j=j: (jnp.bitwise_xor(m[0], j), t * pairs + p))
        for j in range(4)
    ]


def attend(me, proj, rows, heads):
    pairs = -(-heads // 2)
    all_rows = 4 * rows
    tiles = heads * 10 * rows * rows
    return pl.pallas_call(
        partial(attend_kernel, 2 - heads % 2),
        out_shape=(
            jax.ShapeDtypeStruct((all_rows, pairs * 128), BF16),
            jax.ShapeDtypeStruct((pairs, 4, 8, rows), F32),
        ),
        grid_spec=pltpu.PrefetchScalarGridSpec(
            num_scalar_prefetch=1,
            grid=(pairs,),
            in_specs=[s for t in range(3) for s in block_specs(rows, pairs, t)],
            out_specs=[
                pl.BlockSpec((all_rows, 128), lambda p, m: (0, p)),
                pl.BlockSpec((1, 4, 8, rows), lambda p, m: (p, 0, 0, 0)),
            ],
        ),
        cost_estimate=pl.CostEstimate(
            flops=tiles * 4 * HP, bytes_accessed=all_rows * pairs * 1024, transcendentals=tiles
        ),
    )(me, *([proj] * 12))


def attend_back(me, proj, lse, mixed, grad_mixed, rows, heads):
    pairs = -(-heads // 2)
    all_rows = 4 * rows
    tiles = heads * 10 * rows * rows
    return pl.pallas_call(
        partial(attend_back_kernel, 2 - heads % 2),
        out_shape=jax.ShapeDtypeStruct((3, all_rows, pairs * 128), BF16),
        grid_spec=pltpu.PrefetchScalarGridSpec(
            num_scalar_prefetch=1,
            grid=(pairs,),
            in_specs=[s for t in range(3) for s in block_specs(rows, pairs, t)]
            + block_specs(rows, pairs, 0) * 2
            + [pl.BlockSpec((1, 4, 8, rows), lambda p, m: (p, 0, 0, 0))],
            out_specs=pl.BlockSpec((3, all_rows, 128), lambda p, m: (0, 0, p)),
            scratch_shapes=[pltpu.VMEM((4, rows, 128), F32)] * 2,
        ),
        cost_estimate=pl.CostEstimate(
            flops=tiles * 10 * HP, bytes_accessed=all_rows * pairs * 2048, transcendentals=tiles
        ),
    )(me, *([proj] * 12), *([grad_mixed] * 4), *([mixed] * 4), lse)


def make(sizes):
    wide, parts = sizes["wide"], sizes["narrow"]

    def on_device(
        tokens, lengths, norm_one, qkv_weight, out_weight, norm_two, up_weight, down_weight, grad_out
    ):
        cell_count, rows, width = tokens.shape
        own_width = qkv_weight.shape[2]
        heads = own_width // HS
        pad_heads = heads + heads % 2
        pad_width = pad_heads * HP
        units = up_weight.shape[1]
        chunk = -(-max(width, units) // (wide * 16)) * 16
        tall = chunk * wide
        narrow, ring = Narrow(parts), Ring(wide)
        me = lax.axis_index("narrow")
        length = lengths[0]
        own_tokens, own_grad = tokens[0], grad_out[0]
        me_ref = me.reshape(1).astype(jnp.int32)
        own_live = (me * rows + lax.broadcasted_iota(jnp.int32, (rows, 1), 0) < length).astype(F32)

        token_blocks = narrow.gather(own_tokens)
        own_branch = (own_live * own_grad.astype(F32)).astype(BF16)
        out_own, own_branch, token_blocks = lax.optimization_barrier((out_weight, own_branch, token_blocks))
        out_blocks = narrow.gather(out_own)
        grad_blocks = narrow.gather(own_branch)

        def pad_cols(weight):
            split = weight.reshape(width, heads, HS)
            return jnp.pad(split, ((0, 0), (0, pad_heads - heads), (0, HP - HS))).reshape(width, pad_width)

        def pad_rows(weight):
            split = weight.reshape(heads, HS, width)
            return jnp.pad(split, ((0, pad_heads - heads), (0, HP - HS), (0, 0))).reshape(pad_width, width)

        proj = jnp.concatenate([pad_cols(qkv_weight[t]) for t in range(3)], axis=1)
        stream = own_tokens.astype(F32)
        normal_one, rstd_one = layer_stats(stream)
        rows_one = jnp.concatenate(
            [(layer_stats(b.astype(F32))[0] * norm_one).astype(BF16) for b in token_blocks], axis=0
        )
        projected = dot(rows_one, proj, ((1,), (0,))).astype(BF16)
        mixed, lse = attend(me_ref, projected, rows, heads)
        mixed_parts = narrow.exchange([mixed[k * rows : (k + 1) * rows] for k in range(4)])
        mixed_own = jnp.concatenate(mixed_parts, axis=1)
        out_all = jnp.concatenate([pad_rows(b) for b in out_blocks], axis=0)
        middle = stream + own_live * dot(mixed_own, out_all, ((1,), (0,)))
        normal_two, rstd_two = layer_stats(middle)
        rows_two = jnp.concatenate(narrow.gather((normal_two * norm_two).astype(BF16)), axis=0)
        grad_rows = jnp.concatenate(grad_blocks, axis=0)
        pre_act = dot(rows_two, up_weight, ((1,), (0,)))
        grad_hidden = dot(grad_rows, down_weight, ((1,), (1,)))
        cdf = 0.5 * (1.0 + lax.erf(pre_act * 0.5**0.5))
        slope = cdf + pre_act * jnp.exp(-0.5 * pre_act * pre_act) * (0.5 / jnp.pi) ** 0.5
        hidden = (pre_act * cdf).astype(BF16)
        grad_pre = (grad_hidden * slope).astype(BF16)

        def ring_form(left, right):
            left = jnp.pad(left, ((0, 0), (0, tall - left.shape[1])))
            return dot(left, right, ((0,), (0,))).astype(BF16).reshape(wide, chunk, right.shape[1])

        down_sum = ring.total(ring_form(hidden, grad_rows), 1)
        up_sum = ring.total(ring_form(rows_two, grad_pre), -1)
        terms_two = dot(grad_pre, up_weight, ((1,), (1,)))
        grad_normed_two = narrow.scatter_sum(terms_two, rows)
        mlp_terms = dot(hidden, down_weight, ((1,), (0,)))
        mlp_own = narrow.scatter_sum(mlp_terms, rows)
        block_output = (middle + own_live * mlp_own).astype(BF16)

        gain_two = jnp.sum(grad_normed_two * normal_two, axis=0)
        grad_middle = own_grad.astype(F32) + layer_back(grad_normed_two * norm_two, normal_two, rstd_two)
        grad_attn = (own_live * grad_middle).astype(BF16)
        grad_all = dot(grad_attn, out_all, ((1,), (1,))).astype(BF16)
        grad_mixed = jnp.concatenate(
            narrow.exchange([grad_all[:, k * pad_width : (k + 1) * pad_width] for k in range(4)]), axis=0
        )
        attn_rows = jnp.concatenate(narrow.gather(grad_attn), axis=0)
        grad_parts = attend_back(me_ref, projected, lse, mixed, grad_mixed, rows, heads)
        grad_proj = jnp.concatenate([grad_parts[t] for t in range(3)], axis=1)
        terms_one = dot(grad_proj, proj, ((1,), (1,)))
        grad_normed_one = narrow.scatter_sum(terms_one, rows)
        gain_one = jnp.sum(grad_normed_one * normal_one, axis=0)
        grad_stream = layer_back(grad_normed_one * norm_one, normal_one, rstd_one)
        input_grad = (grad_middle + grad_stream).astype(BF16)

        live_width = heads * HP
        left = jnp.concatenate(
            [grad_proj[:, t * pad_width : t * pad_width + live_width] for t in range(3)], axis=1
        )
        last = jnp.concatenate(
            [
                dot(left, rows_one, ((0,), (0,))).astype(BF16),
                dot(mixed[:, :live_width], attn_rows, ((0,), (0,))).astype(BF16),
            ],
            axis=0,
        )
        tail = -(-last.shape[0] // (wide * 16)) * 16
        last = jnp.pad(last, ((0, tail * wide - last.shape[0]), (0, 0))).reshape(wide, tail, width)
        half = tail // 2
        last_sum = jnp.concatenate(
            [ring.total(last[:, :half], 1), ring.total(last[:, half:], -1)], axis=1
        ).reshape(tail * wide, width)

        gains = jnp.stack([gain_one, gain_two])
        for k in (1, 2):
            gains = gains + narrow.send(gains, k)
        hop = 1
        while hop < wide:
            gains = gains + lax.ppermute(gains, "wide", [(i, i ^ hop) for i in range(wide)])
            hop *= 2

        split = last_sum[: 4 * live_width].reshape(4, heads, HP, width)[:, :, :HS]
        qkv_grad = split[:3].reshape(3, own_width, width).transpose(0, 2, 1)
        out_grad = split[3].reshape(own_width, width)
        down_grad = down_sum.reshape(tall, width)[:units]
        up_grad = up_sum.reshape(tall, units)[:width]
        return (
            block_output[None],
            input_grad[None],
            gains[0],
            qkv_grad,
            out_grad,
            gains[1],
            up_grad,
            down_grad,
        )

    return on_device


def solution(mesh):
    in_specs = (
        P("wide", "narrow", None),
        P("wide"),
        P(),
        P(None, None, "narrow"),
        P("narrow", None),
        P(),
        P(None, "narrow"),
        P("narrow", None),
        P("wide", "narrow", None),
    )
    out_specs = (
        P("wide", "narrow", None),
        P("wide", "narrow", None),
        P(),
        P(None, None, "narrow"),
        P("narrow", None),
        P(),
        P(None, "narrow"),
        P("narrow", None),
    )
    return jax.shard_map(
        make(dict(mesh.shape)), mesh=mesh, in_specs=in_specs, out_specs=out_specs, check_vma=False
    )
```

```python
from functools import partial

import jax
import jax.numpy as jnp
from jax import lax
from jax.experimental import pallas as pl
from jax.experimental.pallas import tpu as pltpu
from jax.sharding import PartitionSpec as P

HS = 56
HP = 64
F32 = jnp.float32
BF16 = jnp.bfloat16


def layer_stats(values):
    mean = jnp.mean(values, axis=0, keepdims=True)
    center = values - mean
    spread = jnp.mean(center * center, axis=0, keepdims=True)
    rstd = lax.rsqrt(spread + 1e-05)
    return center * rstd, rstd


def layer_back(grad_scaled, normal, rstd):
    first = jnp.mean(grad_scaled, axis=0, keepdims=True)
    second = jnp.mean(grad_scaled * normal, axis=0, keepdims=True)
    return rstd * (grad_scaled - first - normal * second)


def dot(a, b, dims):
    return lax.dot_general(a, b, (dims, ((), ())), preferred_element_type=F32)


def after(value, *deps):
    return lax.optimization_barrier((value, *deps))[0]


class Narrow:
    def __init__(self, size):
        self.perm = {k: [(i, i ^ k) for i in range(size)] for k in (1, 2, 3)}

    def send(self, value, k):
        return lax.ppermute(value, "narrow", self.perm[k])


class WideSum:
    def __init__(self, size, hops, part):
        self.size, self.hops, self.part, self.rows = size, hops, part, part.shape[0]
        self.step = 0
        index = lax.axis_index("wide")
        bits = [jnp.bitwise_and(index // hop, 1) for hop in hops]
        self.at = jnp.stack(bits).astype(jnp.int32)

    def send(self, value, turn):
        hop = self.hops[turn]
        self.got = lax.ppermute(value, "wide", [(i, i ^ hop) for i in range(self.size)])
        return value

    def advance(self, *deps):
        if self.size != 8:
            if self.step == 0:
                self.whole = lax.psum(self.part.astype(F32), "wide")
            self.step += 1
            return deps[0] if deps else self.part
        got = after(self.got, *deps) if self.step else None
        self.step += 1
        if self.step == 1:
            halves = self.part.reshape(2, self.rows // 2, self.part.shape[1])
            return self.send(lax.dynamic_index_in_dim(halves, 1 - self.at[0], 0, keepdims=False), 0)
        if self.step == 2:
            self.keep, sent = fold(self.at, self.part, got, 1)
            return self.send(sent, 1)
        if self.step == 3:
            self.keep, sent = fold(self.at, self.keep, got, 2)
            return self.send(sent, 2)
        if self.step == 4:
            self.have = (self.keep + got.astype(F32)).astype(BF16)
            return self.send(self.have, 2)
        if self.step == 5:
            self.have = jnp.concatenate([self.have, got], axis=0)
            return self.send(self.have, 1)
        if self.step == 6:
            self.have = jnp.concatenate([self.have, got], axis=0)
            self.send(self.have, 0)
            self.whole = join(self.at, self.have, self.rows, None)
            return self.have
        self.whole = join(self.at, got, self.rows, self.whole)
        return self.whole

    @property
    def done(self):
        return self.step == 7


def fold_kernel(at_ref, keep_ref, sent_ref, got_keep_ref, got_sent_ref, o_keep_ref, o_sent_ref):
    o_keep_ref[...] = keep_ref[...].astype(F32) + got_keep_ref[...].astype(F32)
    o_sent_ref[...] = (sent_ref[...].astype(F32) + got_sent_ref[...].astype(F32)).astype(BF16)


def eighth_of(quarter):
    return -(-quarter // 16) * 8


def fold(at, own, got, turn):
    rows, columns = got.shape
    half = rows // 2 if turn == 1 else eighth_of(rows)
    base = (lambda a: 2 * a[0]) if turn == 1 else (lambda a: 0)
    spec = lambda place: pl.BlockSpec((half, columns), lambda i, a: (place(a), 0))
    return pl.pallas_call(
        fold_kernel,
        out_shape=[
            jax.ShapeDtypeStruct((half, columns), F32),
            jax.ShapeDtypeStruct((half, columns), BF16),
        ],
        grid_spec=pltpu.PrefetchScalarGridSpec(
            num_scalar_prefetch=1,
            grid=(1,),
            in_specs=[
                spec(lambda a: base(a) + a[turn]),
                spec(lambda a: base(a) + 1 - a[turn]),
                spec(lambda a: a[turn]),
                spec(lambda a: 1 - a[turn]),
            ],
            out_specs=[spec(lambda a: 0)] * 2,
        ),
        cost_estimate=pl.CostEstimate(
            flops=rows * columns, bytes_accessed=7 * rows * columns, transcendentals=0
        ),
    )(at, own, own, got, got)


def join_kernel(rows, at_ref, half_ref, *refs):
    o_ref = refs[-1]
    eighth = half_ref.shape[0] // 2
    rest = rows - eighth
    first = at_ref[2] == 0

    @pl.when(first)
    def _():
        o_ref[...] = half_ref[0:rows, :].astype(F32)

    @pl.when(jnp.logical_not(first))
    def _():
        o_ref[0:eighth, :] = half_ref[eighth : 2 * eighth, :].astype(F32)
        o_ref[eighth:rows, :] = half_ref[0:rest, :].astype(F32)


def join(at, half, rows, whole):
    columns, quarter = half.shape[1], rows // 4
    place = (lambda a: a[0]) if whole is None else (lambda a: 1 - a[0])
    return pl.pallas_call(
        partial(join_kernel, quarter),
        out_shape=jax.ShapeDtypeStruct((rows, columns), F32),
        grid_spec=pltpu.PrefetchScalarGridSpec(
            num_scalar_prefetch=1,
            grid=(2,),
            in_specs=[
                pl.BlockSpec((half.shape[0] // 2, columns), lambda i, a: (jnp.bitwise_xor(i, a[1]), 0))
            ]
            + ([] if whole is None else [pl.BlockSpec(memory_space=pl.ANY)]),
            out_specs=pl.BlockSpec((quarter, columns), lambda i, a: (2 * place(a) + i, 0)),
        ),
        input_output_aliases={} if whole is None else {2: 0},
        cost_estimate=pl.CostEstimate(flops=0, bytes_accessed=3 * rows * columns, transcendentals=0),
    )(at, half, *([] if whole is None else [whole]))


LOG2E = 1.4426950408889634
SCALE = HS**-0.5


def nt(a, b):
    return lax.dot_general(a, b, (((1,), (1,)), ((), ())), preferred_element_type=F32)


def nn(a, b):
    return lax.dot_general(a, b, (((1,), (0,)), ((), ())), preferred_element_type=F32)


def half_of(values, which):
    lane = lax.broadcasted_iota(jnp.int32, values.shape, 1)
    keep = lane < HP if which == 0 else lane >= HP
    return jnp.where(keep, values, jnp.zeros_like(values))


def causal_tile(rows):
    key = lax.broadcasted_iota(jnp.int32, (rows, rows), 0)
    query = lax.broadcasted_iota(jnp.int32, (rows, rows), 1)
    return key <= query


def swap_halves(values):
    return pltpu.roll(values.astype(F32), HP, 1).astype(BF16)


def pair_operands(first, second, third, heads):
    if heads == 2:
        return first, second, third
    lone = half_of(second, 0)
    return half_of(first, 0), half_of(swap_halves(first), 0), lone


def attend_kernel(lone_last, me_ref, *refs):
    first, second, third, (o_ref, lse_ref) = refs[0:4], refs[4:8], refs[8:12], refs[12:14]
    me = me_ref[0]
    rows = first[0].shape[0]

    def body(heads):
        tiles = [pair_operands(first[j][...], second[j][...], third[j][...], heads) for j in range(4)]
        value_t = [tiles[j][2].T for j in range(4)]
        causal = causal_tile(rows)
        for a in range(4):
            outs = []
            for h in range(heads):
                query = half_of(tiles[a][0], h)
                score = [nt(tiles[j][1], query) for j in range(a + 1)]
                score[a] = jnp.where(causal, score[a], -1e30)
                top = jnp.max(score[0], axis=0, keepdims=True)
                for j in range(1, a + 1):
                    top = jnp.maximum(top, jnp.max(score[j], axis=0, keepdims=True))
                top = top * (SCALE * LOG2E)
                total = jnp.zeros((1, rows), F32)
                acc = jnp.zeros((HP, rows), F32)
                for j in range(a + 1):
                    p = jnp.exp2(score[j] * (SCALE * LOG2E) - top)
                    total = total + jnp.sum(p, axis=0, keepdims=True)
                    acc = acc + nn(value_t[j][h * HP : (h + 1) * HP], p.astype(BF16))
                outs.append(acc / total)
                lse_ref[0, a, h : h + 1, :] = top + jnp.log2(total)
            if heads == 1:
                outs.append(jnp.zeros((HP, rows), F32))
            at = pl.multiple_of(slot_of(me, a) * rows, rows)
            o_ref[pl.ds(at, rows), :] = jnp.concatenate(outs, axis=0).T.astype(BF16)

    if not lone_last:
        body(2)
        return
    last = pl.num_programs(0) - 1

    @pl.when(pl.program_id(0) < last)
    def _():
        body(2)

    @pl.when(pl.program_id(0) == last)
    def _():
        body(1)


def attend_back_body(heads, me_ref, refs):
    first, second, third, do, o = (refs[4 * i : 4 * i + 4] for i in range(5))
    lse_ref, g_ref, dk_acc, dv_acc = refs[20:24]
    me = me_ref[0]
    rows = first[0].shape[0]
    tiles = [pair_operands(first[j][...], second[j][...], third[j][...], heads) for j in range(4)]
    key_t = [tiles[j][1].T for j in range(4)]
    causal = causal_tile(rows)
    grads_q = []
    for a in range(4):
        grad = do[a][...]
        product = (grad.astype(F32) * o[a][...].astype(F32)).T
        parts = []
        for h in range(heads):
            query, grad_h = half_of(tiles[a][0], h), half_of(grad, h)
            inner = jnp.sum(product[h * HP : (h + 1) * HP], axis=0, keepdims=True)
            lse = lse_ref[0, a, h : h + 1, :]
            dq = jnp.zeros((HP, rows), F32)
            for j in range(a + 1):
                score = nt(tiles[j][1], query) * (SCALE * LOG2E) - lse
                if j == a:
                    score = jnp.where(causal, score, -1e30)
                p = jnp.exp2(score)
                ds = (p * (nt(tiles[j][2], grad_h) - inner)).astype(BF16)
                dv, dk = nn(p.astype(BF16), grad_h), nn(ds, query)
                if a == j and h == 0:
                    dv_acc[j], dk_acc[j] = dv, dk
                else:
                    dv_acc[j] = dv_acc[j] + dv
                    dk_acc[j] = dk_acc[j] + dk
                dq = dq + nn(key_t[j][h * HP : (h + 1) * HP], ds)
            parts.append(dq * SCALE)
        if heads == 1:
            parts.append(jnp.zeros((HP, rows), F32))
        grads_q.append(jnp.concatenate(parts, axis=0).T)
    for j in range(4):
        at = pl.multiple_of(slot_of(me, j) * rows, rows)
        if heads == 2:
            g_ref[pl.ds(at, rows), 0:128] = grads_q[j].astype(BF16)
            g_ref[pl.ds(at, rows), 128:256] = (dk_acc[j] * SCALE).astype(BF16)
            g_ref[pl.ds(at, rows), 256:384] = dv_acc[j].astype(BF16)
        else:
            both = grads_q[j] + pltpu.roll(dk_acc[j] * SCALE, HP, 1)
            g_ref[pl.ds(at, rows), 0:128] = both.astype(BF16)
            g_ref[pl.ds(at, rows), 128:256] = dv_acc[j].astype(BF16)


def attend_back_kernel(lone_last, me_ref, *refs):
    if not lone_last:
        attend_back_body(2, me_ref, refs)
        return
    last = pl.num_programs(0) - 1

    @pl.when(pl.program_id(0) < last)
    def _():
        attend_back_body(2, me_ref, refs)

    @pl.when(pl.program_id(0) == last)
    def _():
        attend_back_body(1, me_ref, refs)


def slot_of(me, block):
    rel = jnp.bitwise_xor(me, block)
    return jnp.bitwise_or((rel & 1) * 2, rel >> 1)


def block_specs(rows, column):
    return [
        pl.BlockSpec((rows, 128), lambda p, m, j=j: (slot_of(m[0], j), column(p))) for j in range(4)
    ]


def attend(me, proj, rows, heads):
    pairs = -(-heads // 2)
    all_rows = 4 * rows
    tiles = heads * 10 * rows * rows
    last_tile = proj.shape[1] // 128 - 1
    return pl.pallas_call(
        partial(attend_kernel, heads % 2 == 1),
        out_shape=(
            jax.ShapeDtypeStruct((all_rows, pairs * 128), BF16),
            jax.ShapeDtypeStruct((pairs, 4, 8, rows), F32),
        ),
        grid_spec=pltpu.PrefetchScalarGridSpec(
            num_scalar_prefetch=1,
            grid=(pairs,),
            in_specs=[
                s
                for t in range(3)
                for s in block_specs(rows, lambda p, t=t: jnp.minimum(3 * p + t, last_tile))
            ],
            out_specs=[
                pl.BlockSpec((all_rows, 128), lambda p, m: (0, p)),
                pl.BlockSpec((1, 4, 8, rows), lambda p, m: (p, 0, 0, 0)),
            ],
        ),
        cost_estimate=pl.CostEstimate(
            flops=tiles * 4 * HP, bytes_accessed=all_rows * pairs * 1024, transcendentals=tiles
        ),
    )(me, *([proj] * 12))


def attend_back(me, proj, lse, mixed, grad_mixed, rows, heads):
    pairs = -(-heads // 2)
    all_rows, columns = proj.shape
    tiles = heads * 10 * rows * rows
    last_tile = columns // 128 - 1
    return pl.pallas_call(
        partial(attend_back_kernel, heads % 2 == 1),
        out_shape=jax.ShapeDtypeStruct((all_rows, columns), BF16),
        grid_spec=pltpu.PrefetchScalarGridSpec(
            num_scalar_prefetch=1,
            grid=(pairs,),
            in_specs=[
                s
                for t in range(3)
                for s in block_specs(rows, lambda p, t=t: jnp.minimum(3 * p + t, last_tile))
            ]
            + block_specs(rows, lambda p: p) * 2
            + [pl.BlockSpec((1, 4, 8, rows), lambda p, m: (p, 0, 0, 0))],
            out_specs=pl.BlockSpec((all_rows, 384), lambda p, m: (0, p)),
            scratch_shapes=[pltpu.VMEM((4, rows, 128), F32)] * 2,
        ),
        cost_estimate=pl.CostEstimate(
            flops=tiles * 10 * HP, bytes_accessed=all_rows * columns * 10, transcendentals=tiles
        ),
    )(me, *([proj] * 12), *([grad_mixed] * 4), *([mixed] * 4), lse)


def make(sizes):
    wide, parts = sizes["wide"], sizes["narrow"]

    def on_device(
        tokens, lengths, norm_one, qkv_weight, out_weight, norm_two, up_weight, down_weight, grad_out
    ):
        cell_count, rows, width = tokens.shape
        own_width = qkv_weight.shape[2]
        heads = own_width // HS
        pairs = -(-heads // 2)
        pad_width = pairs * 128
        narrow = Narrow(parts)
        me = lax.axis_index("narrow")
        me_ref = me.reshape(1).astype(jnp.int32)
        length = lengths[0]
        gain_row_one, gain_row_two = norm_one[:, None], norm_two[:, None]
        own_tokens, own_grad = tokens[0].T, grad_out[0].T
        own_live = (me * rows + lax.broadcasted_iota(jnp.int32, (1, rows), 1) < length).astype(F32)

        tok_y, tok_c = narrow.send(own_tokens, 2), narrow.send(own_tokens, 1)

        full = heads // 2
        split = qkv_weight.transpose(0, 2, 1).reshape(3, heads, HS, width)
        split = jnp.pad(split, ((0, 0), (0, 0), (0, HP - HS), (0, 0)))
        pieces = [split[:, : 2 * full].reshape(3, full, 128, width).transpose(1, 0, 2, 3).reshape(full * 384, width)]
        if heads % 2:
            pieces.append(jnp.pad(split[:, 2 * full].reshape(3 * HP, width), ((0, HP), (0, 0))))
        proj = jnp.concatenate(pieces, axis=0)

        def pad_rows(weight):
            split = weight.reshape(heads, HS, width)
            return jnp.pad(split, ((0, 2 * pairs - heads), (0, HP - HS), (0, 0))).reshape(pad_width, width)

        stream = own_tokens.astype(F32)
        normal_one, rstd_one = layer_stats(stream)

        def first_norm(block):
            return (layer_stats(block.astype(F32))[0] * gain_row_one).astype(BF16)

        near = [first_norm(own_tokens), first_norm(tok_c)]
        tok_y = after(tok_y, proj, *near)
        tok_d = narrow.send(tok_y, 1)
        out_y = narrow.send(after(out_weight, tok_y), 2)
        out_c = narrow.send(after(out_weight, tok_y), 1)
        far_norm = [first_norm(tok_y), first_norm(tok_d)]
        rows_one = jnp.concatenate([near[0], far_norm[0], near[1], far_norm[1]], axis=1)
        projected = dot(rows_one, proj, ((0,), (1,))).astype(BF16)
        own_branch = (own_live * own_grad.astype(F32)).astype(BF16)
        own_branch = after(own_branch, rows_one)
        grad_y, grad_c = narrow.send(own_branch, 2), narrow.send(own_branch, 1)
        mixed, lse = attend(me_ref, projected, rows, heads)
        out_y = after(out_y, mixed)
        out_d = narrow.send(out_y, 1)
        block = lambda a, slot: a[slot * rows : (slot + 1) * rows]
        mixed_y = narrow.send(block(mixed, 1), 2)
        mixed_d = narrow.send(block(mixed, 3), 3)
        mixed_c = narrow.send(block(mixed, 2), 1)
        out_all = [pad_rows(after(b, mixed)) for b in (out_weight, out_y, out_c, out_d)]
        grad_y = after(grad_y, *out_all)
        grad_d = narrow.send(grad_y, 1)
        mixed_y = after(mixed_y, grad_y)
        mixed_own = [block(mixed, 0), mixed_y, mixed_c, mixed_d]
        branch = sum(dot(w, m, ((0,), (1,))) for w, m in zip(out_all, mixed_own))
        middle = stream + own_live * branch
        normal_two, rstd_two = layer_stats(middle)
        own_two = (normal_two * gain_row_two).astype(BF16)
        two_y, two_c = narrow.send(own_two, 2), narrow.send(own_two, 1)
        grad_rows = jnp.concatenate([after(own_branch, own_two), grad_y, grad_c, grad_d], axis=1)
        grad_hidden = dot(down_weight, grad_rows, ((1,), (0,)))
        two_y = after(two_y, grad_hidden)
        two_d = narrow.send(two_y, 1)
        rows_two = jnp.concatenate([own_two, two_y, two_c, two_d], axis=1)
        pre_act = dot(up_weight, rows_two, ((0,), (0,)))
        cdf = 0.5 * (1.0 + lax.erf(pre_act * 0.5**0.5))
        slope = cdf + pre_act * jnp.exp(-0.5 * pre_act * pre_act) * (0.5 / jnp.pi) ** 0.5
        hidden = (pre_act * cdf).astype(BF16)
        grad_pre = (grad_hidden * slope).astype(BF16)

        def wide_sum(hops, part):
            return WideSum(wide, hops, part)

        half = 2 * rows
        down = wide_sum((1, 2, 4), dot(hidden, grad_rows, ((1,), (1,))).astype(BF16))
        mark = down.advance()
        up = wide_sum((2, 1, 4), dot(rows_two, after(grad_pre, mark), ((1,), (1,))).astype(BF16))
        mark = up.advance()

        grad_pre_on = after(grad_pre, mark)
        sent = dot(up_weight, grad_pre_on[:, half:], ((1,), (0,))).astype(BF16)
        got_two = narrow.send(sent, 1)
        kept_two = dot(up_weight, after(grad_pre_on[:, :half], sent), ((1,), (0,)))
        got_two = after(got_two, kept_two).astype(F32)
        far_two = narrow.send((kept_two[:, rows:] + got_two[:, rows:]).astype(BF16), 2)
        near_two = kept_two[:, :rows] + got_two[:, :rows]
        hidden_on = after(hidden, near_two)
        mlp_sent = dot(down_weight, hidden_on[:, half:], ((0,), (0,))).astype(BF16)
        mlp_got = narrow.send(mlp_sent, 1)
        mlp_kept = dot(down_weight, after(hidden_on[:, :half], mlp_sent), ((0,), (0,)))
        mlp_got = after(mlp_got, mlp_kept).astype(F32)
        mlp_far = (mlp_kept[:, rows:] + mlp_got[:, rows:]).astype(BF16)
        mlp_near = mlp_kept[:, :rows] + mlp_got[:, :rows]
        grad_normed_two = near_two + after(far_two, mlp_near, mlp_far).astype(F32)
        gain_two = jnp.sum(grad_normed_two * normal_two, axis=1)
        grad_middle = own_grad.astype(F32) + layer_back(grad_normed_two * gain_row_two, normal_two, rstd_two)
        grad_attn = (own_live * grad_middle).astype(BF16)
        piece = [dot(grad_attn, w, ((0,), (1,))).astype(BF16) for w in out_all]
        mix_y, mix_d, mix_c = narrow.send(piece[1], 2), narrow.send(piece[3], 3), narrow.send(piece[2], 1)
        mark = down.advance(*piece)
        mark = up.advance(mark)
        mix_y = after(mix_y, mark)
        grad_mixed = jnp.concatenate([piece[0], mix_y, mix_c, mix_d], axis=0)
        mark = down.advance(grad_mixed)
        mark = up.advance(mark)
        attn_on = after(grad_attn, mark)
        attn_y, attn_c = narrow.send(attn_on, 2), narrow.send(attn_on, 1)
        grad_proj = attend_back(me_ref, projected, lse, mixed, after(grad_mixed, attn_on), rows, heads)
        attn_y = after(attn_y, grad_proj)
        attn_d = narrow.send(attn_y, 1)
        mlp_send_far = narrow.send(after(mlp_far, attn_y), 2)

        found = dot(grad_proj[:, : 3 * heads * HP], rows_one, ((0,), (1,))).astype(BF16)
        fields = [found[: full * 384].reshape(full, 3, 2, HP, width)[:, :, :, :HS]]
        fields[0] = fields[0].transpose(1, 0, 2, 3, 4).reshape(3, full * 2 * HS, width)
        if heads % 2:
            fields.append(found[full * 384 :].reshape(3, HP, width)[:, :HS])
        qkv_part = jnp.concatenate(fields, axis=1).reshape(3 * own_width, width)
        cut = -(-4 * own_width // 64) * 32
        first = wide_sum((1, 2, 4), qkv_part[:cut])
        mark = first.advance()
        attn_rows = jnp.concatenate([grad_attn, attn_y, attn_c, after(attn_d, mark)], axis=1)
        out_part = dot(mixed[:, : heads * HP], attn_rows, ((0,), (1,))).astype(BF16)
        out_part = out_part.reshape(heads, HP, width)[:, :HS].reshape(own_width, width)
        second = wide_sum((2, 1, 4), jnp.concatenate([qkv_part[cut:], out_part], axis=0))
        mark = second.advance()
        mark = down.advance(mark)
        mark = up.advance(mark)
        grad_proj = after(grad_proj, mark)
        one_sent = dot(proj, grad_proj[half:], ((0,), (1,))).astype(BF16)
        one_got = narrow.send(one_sent, 1)
        one_kept = dot(proj, after(grad_proj[:half], one_sent), ((0,), (1,)))
        one_got = after(one_got, one_kept).astype(F32)
        one_far = narrow.send((one_kept[:, rows:] + one_got[:, rows:]).astype(BF16), 2)
        one_near = one_kept[:, :rows] + one_got[:, :rows]
        mlp_own = mlp_near + after(mlp_send_far, one_near).astype(F32)
        block_output = (middle + own_live * mlp_own).astype(BF16)
        mark = first.advance(block_output)
        mark = second.advance(mark)
        grad_normed_one = one_near + after(one_far, mark).astype(F32)
        gain_one = jnp.sum(grad_normed_one * normal_one, axis=1)
        grad_stream = layer_back(grad_normed_one * gain_row_one, normal_one, rstd_one)
        input_grad = (grad_middle + grad_stream).astype(BF16)
        gains = jnp.stack([gain_one, gain_two])
        mark = down.advance(gains, input_grad)
        mark = up.advance(mark)
        mark = first.advance(mark)
        mark = second.advance(mark)
        for k in (1, 2):
            gains = gains + narrow.send(gains, k)
        for s in (down, up, first, second):
            mark = s.advance(mark, gains)
        hop = 1
        while hop < wide:
            got = lax.ppermute(gains, "wide", [(i, i ^ hop) for i in range(wide)])
            gains = gains + after(got, mark)
            for s in (first, second):
                if not s.done:
                    mark = s.advance(mark, gains)
            hop *= 2
        for s in (down, up, first, second):
            while not s.done:
                mark = s.advance(mark)

        low = 3 * own_width - cut
        qkv_grad = jnp.concatenate([first.whole, second.whole[:low]], axis=0)
        qkv_grad = qkv_grad.reshape(3, own_width, width).transpose(0, 2, 1)
        out_grad = second.whole[low:]
        return (
            block_output.T[None],
            input_grad.T[None],
            gains[0],
            qkv_grad,
            out_grad,
            gains[1],
            up.whole,
            down.whole,
        )

    return on_device


def solution(mesh):
    in_specs = (
        P("wide", "narrow", None),
        P("wide"),
        P(),
        P(None, None, "narrow"),
        P("narrow", None),
        P(),
        P(None, "narrow"),
        P("narrow", None),
        P("wide", "narrow", None),
    )
    out_specs = (
        P("wide", "narrow", None),
        P("wide", "narrow", None),
        P(),
        P(None, None, "narrow"),
        P("narrow", None),
        P(),
        P(None, "narrow"),
        P("narrow", None),
    )
    return jax.shard_map(
        make(dict(mesh.shape)), mesh=mesh, in_specs=in_specs, out_specs=out_specs, check_vma=False
    )
```

```python
from functools import partial

import jax
import jax.numpy as jnp
from jax import lax
from jax.experimental import pallas as pl
from jax.experimental.pallas import tpu as pltpu
from jax.sharding import PartitionSpec as P

HS = 56
HP = 64
F32 = jnp.float32
BF16 = jnp.bfloat16


def layer_stats(values):
    mean = jnp.mean(values, axis=0, keepdims=True)
    center = values - mean
    spread = jnp.mean(center * center, axis=0, keepdims=True)
    rstd = lax.rsqrt(spread + 1e-05)
    return center * rstd, rstd


def layer_back(grad_scaled, normal, rstd):
    first = jnp.mean(grad_scaled, axis=0, keepdims=True)
    second = jnp.mean(grad_scaled * normal, axis=0, keepdims=True)
    return rstd * (grad_scaled - first - normal * second)


def dot(a, b, dims):
    return lax.dot_general(a, b, (dims, ((), ())), preferred_element_type=F32)


def after(value, *deps):
    return lax.optimization_barrier((value, *deps))[0]


class Narrow:
    def __init__(self, size):
        self.perm = {k: [(i, i ^ k) for i in range(size)] for k in (1, 2, 3)}

    def send(self, value, k):
        return lax.ppermute(value, "narrow", self.perm[k])


class WideSum:
    def __init__(self, size, hops, part, out_rows=None, last=False):
        self.size, self.hops, self.part, self.rows = size, hops, part, part.shape[0]
        self.out_rows, self.last = out_rows or self.rows, last
        self.step = 0
        index = lax.axis_index("wide")
        bits = [jnp.bitwise_and(index // hop, 1) for hop in hops]
        self.at = jnp.stack(bits).astype(jnp.int32)

    def send(self, value, turn):
        hop = self.hops[turn]
        self.got = lax.ppermute(value, "wide", [(i, i ^ hop) for i in range(self.size)])
        return value

    def advance(self, *deps):
        if self.size != 8:
            if self.step == 0:
                self.whole = lax.psum(self.part.astype(F32), "wide")
            self.step += 1
            return deps[0] if deps else self.part
        got = after(self.got, *deps) if self.step else None
        self.step += 1
        if self.step == 1:
            halves = self.part.reshape(2, self.rows // 2, self.part.shape[1])
            return self.send(lax.dynamic_index_in_dim(halves, 1 - self.at[0], 0, keepdims=False), 0)
        if self.step == 2:
            quarters = self.part.reshape(4, self.rows // 4, self.part.shape[1])
            got = got.reshape(2, self.rows // 4, got.shape[1])
            place = lambda side: lax.dynamic_index_in_dim(
                quarters, 2 * self.at[0] + side, 0, keepdims=False
            ).astype(F32) + lax.dynamic_index_in_dim(got, side, 0, keepdims=False).astype(F32)
            self.keep = place(self.at[1])
            return self.send(place(1 - self.at[1]).astype(BF16), 1)
        if self.step == 3:
            size = eighth_of(self.rows // 4)
            total = self.keep + got.astype(F32)
            first = self.at[2] == 0
            self.keep = jnp.where(first, total[:size], total[-size:])
            return self.send(jnp.where(first, total[-size:], total[:size]).astype(BF16), 2)
        if self.step == 4:
            self.have = (self.keep + got.astype(F32)).astype(BF16)
            return self.send(self.have, 2)
        if self.step == 5:
            self.have = jnp.concatenate([self.have, got], axis=0)
            return self.send(self.have, 1)
        if self.step == 6:
            self.have = jnp.concatenate([self.have, got], axis=0)
            self.send(self.have, 0)
            if not self.last:
                self.whole = join(self.at, self.have, self.rows, self.out_rows, None)
                return self.whole
            return self.have
        if self.last:
            self.other = got
            return got
        self.whole = join(self.at, got, self.rows, self.out_rows, self.whole)
        return self.whole

    @property
    def done(self):
        return self.step == 7


def eighth_of(quarter):
    return -(-quarter // 16) * 8


def join_kernel(rows, at_ref, half_ref, *refs):
    o_ref = refs[-1]
    eighth = half_ref.shape[0] // 2
    first = at_ref[2] == 0

    @pl.when(first)
    def _():
        o_ref[0:eighth, :] = half_ref[0:eighth, :].astype(F32)
        o_ref[rows - eighth : rows, :] = half_ref[eighth : 2 * eighth, :].astype(F32)

    @pl.when(jnp.logical_not(first))
    def _():
        o_ref[0:eighth, :] = half_ref[eighth : 2 * eighth, :].astype(F32)
        o_ref[rows - eighth : rows, :] = half_ref[0:eighth, :].astype(F32)


def join(at, half, rows, out_rows, whole):
    columns, quarter = half.shape[1], rows // 4
    place = (lambda a: a[0]) if whole is None else (lambda a: 1 - a[0])
    return pl.pallas_call(
        partial(join_kernel, quarter),
        out_shape=jax.ShapeDtypeStruct((out_rows, columns), F32),
        grid_spec=pltpu.PrefetchScalarGridSpec(
            num_scalar_prefetch=1,
            grid=(2,),
            in_specs=[
                pl.BlockSpec((half.shape[0] // 2, columns), lambda i, a: (jnp.bitwise_xor(i, a[1]), 0))
            ]
            + ([] if whole is None else [pl.BlockSpec(memory_space=pl.ANY)]),
            out_specs=pl.BlockSpec((quarter, columns), lambda i, a: (2 * place(a) + i, 0)),
        ),
        input_output_aliases={} if whole is None else {2: 0},
        cost_estimate=pl.CostEstimate(flops=0, bytes_accessed=rows, transcendentals=0),
    )(at, half, *([] if whole is None else [whole]))


def join_last_kernel(rows, at_ref, own_ref, other_ref, whole_ref, o_whole_ref, o_rest_ref):
    eighth = own_ref.shape[0] // 2
    step = pl.program_id(0)
    for mine, half_ref in ((True, own_ref), (False, other_ref)):
        for tail, o_ref in ((0, o_whole_ref), (1, o_rest_ref)):
            for bit in (0, 1):
                here = (step // 2 == tail) & ((at_ref[0] == tail) == mine) & (at_ref[2] == bit)

                @pl.when(here)
                def _(half_ref=half_ref, o_ref=o_ref, bit=bit):
                    low, high = (0, eighth) if bit == 0 else (eighth, 0)
                    o_ref[0:eighth, :] = half_ref[low : low + eighth, :].astype(F32)
                    o_ref[rows - eighth : rows, :] = half_ref[high : high + eighth, :].astype(F32)


def join_last(at, own, other, whole, rows, rest_rows):
    columns, quarter = own.shape[1], rows // 4
    half = pl.BlockSpec((own.shape[0] // 2, columns), lambda i, a: (jnp.bitwise_xor(i & 1, a[1]), 0))
    return pl.pallas_call(
        partial(join_last_kernel, quarter),
        out_shape=[
            jax.ShapeDtypeStruct(whole.shape, F32),
            jax.ShapeDtypeStruct((rest_rows, columns), F32),
        ],
        grid_spec=pltpu.PrefetchScalarGridSpec(
            num_scalar_prefetch=1,
            grid=(4,),
            in_specs=[half, half, pl.BlockSpec(memory_space=pl.ANY)],
            out_specs=[
                pl.BlockSpec((quarter, columns), lambda i, a: (4 + jnp.minimum(i, 1), 0)),
                pl.BlockSpec((quarter, columns), lambda i, a: (jnp.maximum(i - 2, 0), 0)),
            ],
        ),
        input_output_aliases={3: 0},
        cost_estimate=pl.CostEstimate(flops=0, bytes_accessed=rows, transcendentals=0),
    )(at, own, other, whole)


LOG2E = 1.4426950408889634
SCALE = HS**-0.5


def nt(a, b):
    return lax.dot_general(a, b, (((1,), (1,)), ((), ())), preferred_element_type=F32)


def nn(a, b):
    return lax.dot_general(a, b, (((1,), (0,)), ((), ())), preferred_element_type=F32)


def half_of(values, which):
    lane = lax.broadcasted_iota(jnp.int32, values.shape, 1)
    keep = lane < HP if which == 0 else lane >= HP
    return jnp.where(keep, values, jnp.zeros_like(values))


def causal_tile(rows):
    key = lax.broadcasted_iota(jnp.int32, (rows, rows), 0)
    query = lax.broadcasted_iota(jnp.int32, (rows, rows), 1)
    return key <= query


def swap_halves(values):
    return pltpu.roll(values.astype(F32), HP, 1).astype(BF16)


def pair_operands(first, second, third, heads):
    if heads == 2:
        return first, second, third
    lone = half_of(second, 0)
    return half_of(first, 0), half_of(swap_halves(first), 0), lone


def attend_kernel(lone_last, me_ref, *refs):
    first, second, third, (o_ref, lse_ref) = refs[0:4], refs[4:8], refs[8:12], refs[12:14]
    me = me_ref[0]
    rows = first[0].shape[0]

    def body(heads):
        tiles = [pair_operands(first[j][...], second[j][...], third[j][...], heads) for j in range(4)]
        value_t = [tiles[j][2].T for j in range(4)]
        causal = causal_tile(rows)
        for a in range(4):
            outs = []
            for h in range(heads):
                query = half_of(tiles[a][0], h)
                score = [nt(tiles[j][1], query) for j in range(a + 1)]
                score[a] = jnp.where(causal, score[a], -1e30)
                top = jnp.max(score[0], axis=0, keepdims=True)
                for j in range(1, a + 1):
                    top = jnp.maximum(top, jnp.max(score[j], axis=0, keepdims=True))
                top = top * (SCALE * LOG2E)
                total = jnp.zeros((1, rows), F32)
                acc = jnp.zeros((HP, rows), F32)
                for j in range(a + 1):
                    p = jnp.exp2(score[j] * (SCALE * LOG2E) - top)
                    total = total + jnp.sum(p, axis=0, keepdims=True)
                    acc = acc + nn(value_t[j][h * HP : (h + 1) * HP], p.astype(BF16))
                outs.append(acc / total)
                lse_ref[0, a, h : h + 1, :] = top + jnp.log2(total)
            if heads == 1:
                outs.append(jnp.zeros((HP, rows), F32))
            at = pl.multiple_of(slot_of(me, a) * rows, rows)
            o_ref[pl.ds(at, rows), :] = jnp.concatenate(outs, axis=0).T.astype(BF16)

    if not lone_last:
        body(2)
        return
    last = pl.num_programs(0) - 1

    @pl.when(pl.program_id(0) < last)
    def _():
        body(2)

    @pl.when(pl.program_id(0) == last)
    def _():
        body(1)


def attend_back_body(heads, me_ref, refs):
    first, second, third, do, o = (refs[4 * i : 4 * i + 4] for i in range(5))
    lse_ref, g_ref, dk_acc, dv_acc = refs[20:24]
    me = me_ref[0]
    rows = first[0].shape[0]
    tiles = [pair_operands(first[j][...], second[j][...], third[j][...], heads) for j in range(4)]
    key_t = [tiles[j][1].T for j in range(4)]
    causal = causal_tile(rows)
    grads_q = []
    for a in range(4):
        grad = do[a][...]
        product = (grad.astype(F32) * o[a][...].astype(F32)).T
        parts = []
        for h in range(heads):
            query, grad_h = half_of(tiles[a][0], h), half_of(grad, h)
            inner = jnp.sum(product[h * HP : (h + 1) * HP], axis=0, keepdims=True)
            lse = lse_ref[0, a, h : h + 1, :]
            dq = jnp.zeros((HP, rows), F32)
            for j in range(a + 1):
                score = nt(tiles[j][1], query) * (SCALE * LOG2E) - lse
                if j == a:
                    score = jnp.where(causal, score, -1e30)
                p = jnp.exp2(score)
                ds = (p * (nt(tiles[j][2], grad_h) - inner)).astype(BF16)
                dv, dk = nn(p.astype(BF16), grad_h), nn(ds, query)
                if a == j and h == 0:
                    dv_acc[j], dk_acc[j] = dv, dk
                else:
                    dv_acc[j] = dv_acc[j] + dv
                    dk_acc[j] = dk_acc[j] + dk
                dq = dq + nn(key_t[j][h * HP : (h + 1) * HP], ds)
            parts.append(dq * SCALE)
        if heads == 1:
            parts.append(jnp.zeros((HP, rows), F32))
        grads_q.append(jnp.concatenate(parts, axis=0).T)
    for j in range(4):
        at = pl.multiple_of(slot_of(me, j) * rows, rows)
        if heads == 2:
            g_ref[pl.ds(at, rows), 0:128] = grads_q[j].astype(BF16)
            g_ref[pl.ds(at, rows), 128:256] = (dk_acc[j] * SCALE).astype(BF16)
            g_ref[pl.ds(at, rows), 256:384] = dv_acc[j].astype(BF16)
        else:
            both = grads_q[j] + pltpu.roll(dk_acc[j] * SCALE, HP, 1)
            g_ref[pl.ds(at, rows), 0:128] = both.astype(BF16)
            g_ref[pl.ds(at, rows), 128:256] = dv_acc[j].astype(BF16)


def attend_back_kernel(lone_last, me_ref, *refs):
    if not lone_last:
        attend_back_body(2, me_ref, refs)
        return
    last = pl.num_programs(0) - 1

    @pl.when(pl.program_id(0) < last)
    def _():
        attend_back_body(2, me_ref, refs)

    @pl.when(pl.program_id(0) == last)
    def _():
        attend_back_body(1, me_ref, refs)


def slot_of(me, block):
    rel = jnp.bitwise_xor(me, block)
    return jnp.bitwise_or((rel & 1) * 2, rel >> 1)


def block_specs(rows, column):
    return [
        pl.BlockSpec((rows, 128), lambda p, m, j=j: (slot_of(m[0], j), column(p))) for j in range(4)
    ]


def attend(me, proj, rows, heads):
    pairs = -(-heads // 2)
    all_rows = 4 * rows
    last_tile = proj.shape[1] // 128 - 1
    return pl.pallas_call(
        partial(attend_kernel, heads % 2 == 1),
        out_shape=(
            jax.ShapeDtypeStruct((all_rows, pairs * 128), BF16),
            jax.ShapeDtypeStruct((pairs, 4, 8, rows), F32),
        ),
        grid_spec=pltpu.PrefetchScalarGridSpec(
            num_scalar_prefetch=1,
            grid=(pairs,),
            in_specs=[
                s
                for t in range(3)
                for s in block_specs(rows, lambda p, t=t: jnp.minimum(3 * p + t, last_tile))
            ],
            out_specs=[
                pl.BlockSpec((all_rows, 128), lambda p, m: (0, p)),
                pl.BlockSpec((1, 4, 8, rows), lambda p, m: (p, 0, 0, 0)),
            ],
        ),
        cost_estimate=pl.CostEstimate(
            flops=rows, bytes_accessed=rows, transcendentals=0
        ),
    )(me, *([proj] * 12))


def attend_back(me, proj, lse, mixed, grad_mixed, rows, heads):
    pairs = -(-heads // 2)
    all_rows, columns = proj.shape
    last_tile = columns // 128 - 1
    return pl.pallas_call(
        partial(attend_back_kernel, heads % 2 == 1),
        out_shape=jax.ShapeDtypeStruct((all_rows, columns), BF16),
        grid_spec=pltpu.PrefetchScalarGridSpec(
            num_scalar_prefetch=1,
            grid=(pairs,),
            in_specs=[
                s
                for t in range(3)
                for s in block_specs(rows, lambda p, t=t: jnp.minimum(3 * p + t, last_tile))
            ]
            + block_specs(rows, lambda p: p) * 2
            + [pl.BlockSpec((1, 4, 8, rows), lambda p, m: (p, 0, 0, 0))],
            out_specs=pl.BlockSpec((all_rows, 384), lambda p, m: (0, p)),
            scratch_shapes=[pltpu.VMEM((4, rows, 128), F32)] * 2,
        ),
        cost_estimate=pl.CostEstimate(
            flops=rows, bytes_accessed=rows, transcendentals=0
        ),
    )(me, *([proj] * 12), *([grad_mixed] * 4), *([mixed] * 4), lse)


def make(sizes):
    wide, parts = sizes["wide"], sizes["narrow"]

    def on_device(
        tokens, lengths, norm_one, qkv_weight, out_weight, norm_two, up_weight, down_weight, grad_out
    ):
        cell_count, rows, width = tokens.shape
        own_width = qkv_weight.shape[2]
        heads = own_width // HS
        pairs = -(-heads // 2)
        pad_width = pairs * 128
        narrow = Narrow(parts)
        me = lax.axis_index("narrow")
        me_ref = me.reshape(1).astype(jnp.int32)
        length = lengths[0]
        gain_row_one, gain_row_two = norm_one[:, None], norm_two[:, None]
        own_tokens, own_grad = tokens[0].T, grad_out[0].T
        own_live = (me * rows + lax.broadcasted_iota(jnp.int32, (1, rows), 1) < length).astype(F32)

        tok_y, tok_c = narrow.send(own_tokens, 2), narrow.send(own_tokens, 1)

        full = heads // 2
        split = qkv_weight.transpose(0, 2, 1).reshape(3, heads, HS, width)
        split = jnp.pad(split, ((0, 0), (0, 0), (0, HP - HS), (0, 0)))
        pieces = [split[:, : 2 * full].reshape(3, full, 128, width).transpose(1, 0, 2, 3).reshape(full * 384, width)]
        if heads % 2:
            pieces.append(jnp.pad(split[:, 2 * full].reshape(3 * HP, width), ((0, HP), (0, 0))))
        proj = jnp.concatenate(pieces, axis=0)

        def pad_rows(weight):
            split = weight.reshape(heads, HS, width)
            return jnp.pad(split, ((0, 2 * pairs - heads), (0, HP - HS), (0, 0))).reshape(pad_width, width)

        stream = own_tokens.astype(F32)
        normal_one, rstd_one = layer_stats(stream)

        def first_norm(block):
            return (layer_stats(block.astype(F32))[0] * gain_row_one).astype(BF16)

        near = [first_norm(own_tokens), first_norm(tok_c)]
        tok_y = after(tok_y, proj, *near)
        tok_d = narrow.send(tok_y, 1)
        out_y = narrow.send(after(out_weight, tok_y), 2)
        out_c = narrow.send(after(out_weight, tok_y), 1)
        far_norm = [first_norm(tok_y), first_norm(tok_d)]
        rows_one = jnp.concatenate([near[0], far_norm[0], near[1], far_norm[1]], axis=1)
        projected = dot(rows_one, proj, ((0,), (1,))).astype(BF16)
        own_branch = (own_live * own_grad.astype(F32)).astype(BF16)
        own_branch = after(own_branch, tok_y)
        grad_y, grad_c = narrow.send(own_branch, 2), narrow.send(own_branch, 1)
        mixed, lse = attend(me_ref, projected, rows, heads)
        block = lambda a, slot: a[slot * rows : (slot + 1) * rows]
        mixed_y = narrow.send(block(mixed, 1), 2)
        mixed_d = narrow.send(block(mixed, 3), 3)
        mixed_c = narrow.send(block(mixed, 2), 1)
        out_y = after(out_y, mixed)
        out_d = narrow.send(out_y, 1)
        grad_y = after(grad_y, out_y)
        grad_d = narrow.send(grad_y, 1)
        out_all = [pad_rows(after(b, grad_y)) for b in (out_weight, out_y, out_c, out_d)]
        mixed_own = [block(mixed, 0), mixed_y, mixed_c, mixed_d]
        branch = sum(dot(w, m, ((0,), (1,))) for w, m in zip(out_all, mixed_own))
        middle = stream + own_live * branch
        normal_two, rstd_two = layer_stats(middle)
        own_two = (normal_two * gain_row_two).astype(BF16)
        two_y, two_c = narrow.send(own_two, 2), narrow.send(own_two, 1)
        grad_rows = jnp.concatenate([after(own_branch, own_two), grad_y, grad_c, grad_d], axis=1)
        grad_hidden = dot(down_weight, grad_rows, ((1,), (0,)))
        two_y = after(two_y, grad_hidden)
        two_d = narrow.send(two_y, 1)
        rows_two = jnp.concatenate([own_two, two_y, two_c, two_d], axis=1)
        pre_act = dot(up_weight, rows_two, ((0,), (0,)))
        cdf = 0.5 * (1.0 + lax.erf(pre_act * 0.5**0.5))
        slope = cdf + pre_act * jnp.exp(-0.5 * pre_act * pre_act) * (0.5 / jnp.pi) ** 0.5
        hidden = (pre_act * cdf).astype(BF16)
        grad_pre = (grad_hidden * slope).astype(BF16)

        def wide_sum(hops, part):
            return WideSum(wide, hops, part)

        half = 2 * rows
        down = wide_sum((1, 2, 4), dot(hidden, grad_rows, ((1,), (1,))).astype(BF16))
        mark = down.advance()

        grad_pre_on = after(grad_pre, mark)
        sent = dot(up_weight, grad_pre_on[:, half:], ((1,), (0,))).astype(BF16)
        got_two = narrow.send(sent, 1)
        kept_two = dot(up_weight, after(grad_pre_on[:, :half], sent), ((1,), (0,)))
        got_two = after(got_two, kept_two).astype(F32)
        far_sum = (kept_two[:, rows:] + got_two[:, rows:]).astype(BF16)
        far_two = narrow.send(far_sum, 2)
        near_two = kept_two[:, :rows] + got_two[:, :rows]
        up = wide_sum((2, 1, 4), dot(rows_two, after(grad_pre_on, far_sum), ((1,), (1,))).astype(BF16))
        mark = up.advance()
        grad_normed_two = near_two + after(far_two, mark).astype(F32)
        gain_two = jnp.sum(grad_normed_two * normal_two, axis=1)
        grad_middle = own_grad.astype(F32) + layer_back(grad_normed_two * gain_row_two, normal_two, rstd_two)
        grad_attn = (own_live * grad_middle).astype(BF16)
        piece = [dot(grad_attn, w, ((0,), (1,))).astype(BF16) for w in out_all]
        mix_y, mix_d, mix_c = narrow.send(piece[1], 2), narrow.send(piece[3], 3), narrow.send(piece[2], 1)
        hidden_on = after(hidden, *piece)
        mlp_sent = dot(down_weight, hidden_on[:, half:], ((0,), (0,))).astype(BF16)
        mlp_got = narrow.send(mlp_sent, 1)
        mlp_kept = dot(down_weight, after(hidden_on[:, :half], mlp_sent), ((0,), (0,)))
        mix_y = after(mix_y, mlp_kept)
        grad_mixed = jnp.concatenate([piece[0], mix_y, mix_c, mix_d], axis=0)
        attn_on = after(grad_attn, grad_mixed)
        attn_y, attn_c = narrow.send(attn_on, 2), narrow.send(attn_on, 1)
        grad_proj = attend_back(me_ref, projected, lse, mixed, after(grad_mixed, attn_on), rows, heads)
        mark = down.advance(grad_proj)
        mark = up.advance(mark)
        grad_proj = after(grad_proj, mark)
        attn_y = after(attn_y, grad_proj)
        attn_d = narrow.send(attn_y, 1)
        mlp_got = after(mlp_got, attn_y).astype(F32)
        mlp_far = (mlp_kept[:, rows:] + mlp_got[:, rows:]).astype(BF16)
        mlp_near = mlp_kept[:, :rows] + mlp_got[:, :rows]
        mlp_send_far = narrow.send(after(mlp_far, attn_y), 2)

        found = dot(grad_proj[:, : 3 * heads * HP], rows_one, ((0,), (1,))).astype(BF16)
        fields = [found[: full * 384].reshape(full, 3, 2, HP, width)[:, :, :, :HS]]
        fields[0] = fields[0].transpose(1, 0, 2, 3, 4).reshape(3, full * 2 * HS, width)
        if heads % 2:
            fields.append(found[full * 384 :].reshape(3, HP, width)[:, :HS])
        qkv_part = jnp.concatenate(fields, axis=1).reshape(3 * own_width, width)
        cut = -(-own_width // 16) * 32
        low = 3 * own_width - cut
        filled = lambda a: jnp.pad(a, ((0, cut // 2 - a.shape[0]), (0, 0)))
        first = WideSum(wide, (1, 2, 4), qkv_part[:cut], 3 * own_width)
        mark = first.advance()
        mark = down.advance(mark)
        mark = up.advance(mark)
        attn_rows = jnp.concatenate([grad_attn, attn_y, attn_c, after(attn_d, mark)], axis=1)
        out_part = dot(mixed[:, : heads * HP], attn_rows, ((0,), (1,))).astype(BF16)
        out_part = out_part.reshape(heads, HP, width)[:, :HS].reshape(own_width, width)
        second_part = jnp.concatenate([filled(qkv_part[cut:]), filled(out_part)], axis=0)
        second = WideSum(wide, (2, 1, 4), second_part, last=True)
        mark = second.advance()
        mark = down.advance(mark)
        mark = up.advance(mark)
        grad_proj = after(grad_proj, mark)
        one_sent = dot(proj, grad_proj[half:], ((0,), (1,))).astype(BF16)
        one_got = narrow.send(one_sent, 1)
        one_kept = dot(proj, after(grad_proj[:half], one_sent), ((0,), (1,)))
        one_got = after(one_got, one_kept).astype(F32)
        one_sum = (one_kept[:, rows:] + one_got[:, rows:]).astype(BF16)
        one_far = narrow.send(one_sum, 2)
        one_near = one_kept[:, :rows] + one_got[:, :rows]
        mark = first.advance(one_sum)
        mark = second.advance(mark)
        mlp_own = mlp_near + after(mlp_send_far, mark).astype(F32)
        block_output = (middle + own_live * mlp_own).astype(BF16)
        grad_normed_one = one_near + after(one_far, block_output).astype(F32)
        gain_one = jnp.sum(grad_normed_one * normal_one, axis=1)
        grad_stream = layer_back(grad_normed_one * gain_row_one, normal_one, rstd_one)
        input_grad = (grad_middle + grad_stream).astype(BF16)
        gains = jnp.stack([gain_one, gain_two])
        for hop in (1, 2):
            gains = gains + narrow.send(gains, hop)
        mark = gains
        turns = [[first, second, down, up], [first, second, down], [first, second]]
        order = (4, 1, 2) + tuple(8 * 2**i for i in range(wide.bit_length() - 4))
        for hop in order:
            got = lax.ppermute(gains, "wide", [(i, i ^ hop) for i in range(wide)])
            for s in turns.pop(0) if turns else ():
                mark = s.advance(mark, gains)
            gains = gains + after(got, mark)
        mark = up.advance(mark, gains)
        for s in (first, second, down, up, first, second):
            mark = s.advance(mark)

        if wide == 8:
            qkv_grad, out_grad = join_last(
                second.at, second.have, second.other, first.whole, second.rows, own_width
            )
        else:
            qkv_grad = jnp.concatenate([first.whole, second.whole[:low]], axis=0)
            out_grad = second.whole[cut // 2 : cut // 2 + own_width]
        qkv_grad = qkv_grad.reshape(3, own_width, width).transpose(0, 2, 1)
        return (
            block_output.T[None],
            input_grad.T[None],
            gains[0],
            qkv_grad,
            out_grad,
            gains[1],
            up.whole,
            down.whole,
        )

    return on_device


def solution(mesh):
    in_specs = (
        P("wide", "narrow", None),
        P("wide"),
        P(),
        P(None, None, "narrow"),
        P("narrow", None),
        P(),
        P(None, "narrow"),
        P("narrow", None),
        P("wide", "narrow", None),
    )
    out_specs = (
        P("wide", "narrow", None),
        P("wide", "narrow", None),
        P(),
        P(None, None, "narrow"),
        P("narrow", None),
        P(),
        P(None, "narrow"),
        P("narrow", None),
    )
    return jax.shard_map(
        make(dict(mesh.shape)), mesh=mesh, in_specs=in_specs, out_specs=out_specs, check_vma=False
    )
```

```python
from functools import partial

import jax
import jax.numpy as jnp
from jax import lax
from jax.experimental import pallas as pl
from jax.experimental.pallas import tpu as pltpu
from jax.sharding import PartitionSpec as P

HS = 56
HP = 64
F32 = jnp.float32
BF16 = jnp.bfloat16


def layer_stats(values):
    mean = jnp.mean(values, axis=0, keepdims=True)
    center = values - mean
    spread = jnp.mean(center * center, axis=0, keepdims=True)
    rstd = lax.rsqrt(spread + 1e-05)
    return center * rstd, rstd


def layer_back(grad_scaled, normal, rstd):
    first = jnp.mean(grad_scaled, axis=0, keepdims=True)
    second = jnp.mean(grad_scaled * normal, axis=0, keepdims=True)
    return rstd * (grad_scaled - first - normal * second)


def dot(a, b, dims):
    return lax.dot_general(a, b, (dims, ((), ())), preferred_element_type=F32)


def after(value, *deps):
    return lax.optimization_barrier((value, *deps))[0]


class Narrow:
    def __init__(self, size):
        self.perm = {k: [(i, i ^ k) for i in range(size)] for k in (1, 2, 3)}

    def send(self, value, k):
        return lax.ppermute(value, "narrow", self.perm[k])


class WideSum:
    def __init__(self, size, hops, part, out_rows=None, last=False):
        self.size, self.hops, self.part, self.rows = size, hops, part, part.shape[0]
        self.out_rows, self.last = out_rows or self.rows, last
        self.step = 0
        index = lax.axis_index("wide")
        bits = [jnp.bitwise_and(index // hop, 1) for hop in hops]
        self.at = jnp.stack(bits).astype(jnp.int32)

    def send(self, value, turn):
        hop = self.hops[turn]
        self.got = lax.ppermute(value, "wide", [(i, i ^ hop) for i in range(self.size)])
        return value

    def advance(self, *deps):
        if self.size != 8:
            if self.step == 0:
                self.whole = lax.psum(self.part.astype(F32), "wide")
            self.step += 1
            return deps[0] if deps else self.part
        got = after(self.got, *deps) if self.step else None
        self.step += 1
        if self.step == 1:
            halves = self.part.reshape(2, self.rows // 2, self.part.shape[1])
            return self.send(lax.dynamic_index_in_dim(halves, 1 - self.at[0], 0, keepdims=False), 0)
        if self.step == 2:
            quarters = self.part.reshape(4, self.rows // 4, self.part.shape[1])
            got = got.reshape(2, self.rows // 4, got.shape[1])
            place = lambda side: lax.dynamic_index_in_dim(
                quarters, 2 * self.at[0] + side, 0, keepdims=False
            ).astype(F32) + lax.dynamic_index_in_dim(got, side, 0, keepdims=False).astype(F32)
            self.keep = place(self.at[1])
            return self.send(place(1 - self.at[1]).astype(BF16), 1)
        if self.step == 3:
            size = eighth_of(self.rows // 4)
            total = self.keep + got.astype(F32)
            first = self.at[2] == 0
            self.keep = jnp.where(first, total[:size], total[-size:])
            return self.send(jnp.where(first, total[-size:], total[:size]).astype(BF16), 2)
        if self.step == 4:
            self.have = (self.keep + got.astype(F32)).astype(BF16)
            return self.send(self.have, 2)
        if self.step == 5:
            self.have = jnp.concatenate([self.have, got], axis=0)
            return self.send(self.have, 1)
        if self.step == 6:
            self.have = jnp.concatenate([self.have, got], axis=0)
            self.send(self.have, 0)
            if not self.last:
                self.whole = join(self.at, self.have, self.rows, self.out_rows, None)
                return self.whole
            return self.have
        if self.last:
            self.other = got
            return got
        self.whole = join(self.at, got, self.rows, self.out_rows, self.whole)
        return self.whole

    @property
    def done(self):
        return self.step == 7


def eighth_of(quarter):
    return -(-quarter // 16) * 8


def join_kernel(rows, at_ref, half_ref, *refs):
    o_ref = refs[-1]
    eighth = half_ref.shape[0] // 2
    first = at_ref[2] == 0

    @pl.when(first)
    def _():
        o_ref[0:eighth, :] = half_ref[0:eighth, :].astype(F32)
        o_ref[rows - eighth : rows, :] = half_ref[eighth : 2 * eighth, :].astype(F32)

    @pl.when(jnp.logical_not(first))
    def _():
        o_ref[0:eighth, :] = half_ref[eighth : 2 * eighth, :].astype(F32)
        o_ref[rows - eighth : rows, :] = half_ref[0:eighth, :].astype(F32)


def join(at, half, rows, out_rows, whole):
    columns, quarter = half.shape[1], rows // 4
    place = (lambda a: a[0]) if whole is None else (lambda a: 1 - a[0])
    return pl.pallas_call(
        partial(join_kernel, quarter),
        out_shape=jax.ShapeDtypeStruct((out_rows, columns), F32),
        grid_spec=pltpu.PrefetchScalarGridSpec(
            num_scalar_prefetch=1,
            grid=(2,),
            in_specs=[
                pl.BlockSpec((half.shape[0] // 2, columns), lambda i, a: (jnp.bitwise_xor(i, a[1]), 0))
            ]
            + ([] if whole is None else [pl.BlockSpec(memory_space=pl.ANY)]),
            out_specs=pl.BlockSpec((quarter, columns), lambda i, a: (2 * place(a) + i, 0)),
        ),
        input_output_aliases={} if whole is None else {2: 0},
        cost_estimate=pl.CostEstimate(flops=0, bytes_accessed=rows, transcendentals=0),
    )(at, half, *([] if whole is None else [whole]))


def join_last_kernel(rows, at_ref, own_ref, other_ref, whole_ref, o_whole_ref, o_rest_ref):
    eighth = own_ref.shape[0] // 2
    step = pl.program_id(0)
    for mine, half_ref in ((True, own_ref), (False, other_ref)):
        for tail, o_ref in ((0, o_whole_ref), (1, o_rest_ref)):
            for bit in (0, 1):
                here = (step // 2 == tail) & ((at_ref[0] == tail) == mine) & (at_ref[2] == bit)

                @pl.when(here)
                def _(half_ref=half_ref, o_ref=o_ref, bit=bit):
                    low, high = (0, eighth) if bit == 0 else (eighth, 0)
                    o_ref[0:eighth, :] = half_ref[low : low + eighth, :].astype(F32)
                    o_ref[rows - eighth : rows, :] = half_ref[high : high + eighth, :].astype(F32)


def join_last(at, own, other, whole, rows, rest_rows):
    columns, quarter = own.shape[1], rows // 4
    half = pl.BlockSpec((own.shape[0] // 2, columns), lambda i, a: (jnp.bitwise_xor(i & 1, a[1]), 0))
    return pl.pallas_call(
        partial(join_last_kernel, quarter),
        out_shape=[
            jax.ShapeDtypeStruct(whole.shape, F32),
            jax.ShapeDtypeStruct((rest_rows, columns), F32),
        ],
        grid_spec=pltpu.PrefetchScalarGridSpec(
            num_scalar_prefetch=1,
            grid=(4,),
            in_specs=[half, half, pl.BlockSpec(memory_space=pl.ANY)],
            out_specs=[
                pl.BlockSpec((quarter, columns), lambda i, a: (4 + jnp.minimum(i, 1), 0)),
                pl.BlockSpec((quarter, columns), lambda i, a: (jnp.maximum(i - 2, 0), 0)),
            ],
        ),
        input_output_aliases={3: 0},
        cost_estimate=pl.CostEstimate(flops=0, bytes_accessed=rows, transcendentals=0),
    )(at, own, other, whole)


LOG2E = 1.4426950408889634
SCALE = HS**-0.5


def nt(a, b):
    return lax.dot_general(a, b, (((1,), (1,)), ((), ())), preferred_element_type=F32)


def nn(a, b):
    return lax.dot_general(a, b, (((1,), (0,)), ((), ())), preferred_element_type=F32)


def half_of(values, which):
    lane = lax.broadcasted_iota(jnp.int32, values.shape, 1)
    keep = lane < HP if which == 0 else lane >= HP
    return jnp.where(keep, values, jnp.zeros_like(values))


def causal_tile(rows):
    key = lax.broadcasted_iota(jnp.int32, (rows, rows), 0)
    query = lax.broadcasted_iota(jnp.int32, (rows, rows), 1)
    return key <= query


def swap_halves(values):
    return pltpu.roll(values.astype(F32), HP, 1).astype(BF16)


def pair_operands(first, second, third, heads):
    if heads == 2:
        return first, second, third
    lone = half_of(second, 0)
    return half_of(first, 0), half_of(swap_halves(first), 0), lone


def attend_kernel(lone_last, me_ref, *refs):
    first, second, third, (o_ref, lse_ref) = refs[0:4], refs[4:8], refs[8:12], refs[12:14]
    me = me_ref[0]
    rows = first[0].shape[0]

    def body(heads):
        tiles = [pair_operands(first[j][...], second[j][...], third[j][...], heads) for j in range(4)]
        value_t = [tiles[j][2].T for j in range(4)]
        causal = causal_tile(rows)
        for a in range(4):
            outs = []
            for h in range(heads):
                query = half_of(tiles[a][0], h)
                score = [nt(tiles[j][1], query) for j in range(a + 1)]
                score[a] = jnp.where(causal, score[a], -1e30)
                top = jnp.max(score[0], axis=0, keepdims=True)
                for j in range(1, a + 1):
                    top = jnp.maximum(top, jnp.max(score[j], axis=0, keepdims=True))
                top = top * (SCALE * LOG2E)
                total = jnp.zeros((1, rows), F32)
                acc = jnp.zeros((HP, rows), F32)
                for j in range(a + 1):
                    p = jnp.exp2(score[j] * (SCALE * LOG2E) - top)
                    total = total + jnp.sum(p, axis=0, keepdims=True)
                    acc = acc + nn(value_t[j][h * HP : (h + 1) * HP], p.astype(BF16))
                outs.append(acc / total)
                lse_ref[0, a, h : h + 1, :] = top + jnp.log2(total)
            if heads == 1:
                outs.append(jnp.zeros((HP, rows), F32))
            at = pl.multiple_of(slot_of(me, a) * rows, rows)
            o_ref[pl.ds(at, rows), :] = jnp.concatenate(outs, axis=0).T.astype(BF16)

    if not lone_last:
        body(2)
        return
    last = pl.num_programs(0) - 1

    @pl.when(pl.program_id(0) < last)
    def _():
        body(2)

    @pl.when(pl.program_id(0) == last)
    def _():
        body(1)


def attend_back_body(heads, me_ref, refs):
    first, second, third, do, o = (refs[4 * i : 4 * i + 4] for i in range(5))
    lse_ref, g_ref, dk_acc, dv_acc = refs[20:24]
    me = me_ref[0]
    rows = first[0].shape[0]
    tiles = [pair_operands(first[j][...], second[j][...], third[j][...], heads) for j in range(4)]
    key_t = [tiles[j][1].T for j in range(4)]
    causal = causal_tile(rows)
    grads_q = []
    for a in range(4):
        grad = do[a][...]
        product = (grad.astype(F32) * o[a][...].astype(F32)).T
        parts = []
        for h in range(heads):
            query, grad_h = half_of(tiles[a][0], h), half_of(grad, h)
            inner = jnp.sum(product[h * HP : (h + 1) * HP], axis=0, keepdims=True)
            lse = lse_ref[0, a, h : h + 1, :]
            dq = jnp.zeros((HP, rows), F32)
            for j in range(a + 1):
                score = nt(tiles[j][1], query) * (SCALE * LOG2E) - lse
                if j == a:
                    score = jnp.where(causal, score, -1e30)
                p = jnp.exp2(score)
                ds = (p * (nt(tiles[j][2], grad_h) - inner)).astype(BF16)
                dv, dk = nn(p.astype(BF16), grad_h), nn(ds, query)
                if a == j and h == 0:
                    dv_acc[j], dk_acc[j] = dv, dk
                else:
                    dv_acc[j] = dv_acc[j] + dv
                    dk_acc[j] = dk_acc[j] + dk
                dq = dq + nn(key_t[j][h * HP : (h + 1) * HP], ds)
            parts.append(dq * SCALE)
        if heads == 1:
            parts.append(jnp.zeros((HP, rows), F32))
        grads_q.append(jnp.concatenate(parts, axis=0).T)
    for j in range(4):
        at = pl.multiple_of(slot_of(me, j) * rows, rows)
        if heads == 2:
            g_ref[pl.ds(at, rows), 0:128] = grads_q[j].astype(BF16)
            g_ref[pl.ds(at, rows), 128:256] = (dk_acc[j] * SCALE).astype(BF16)
            g_ref[pl.ds(at, rows), 256:384] = dv_acc[j].astype(BF16)
        else:
            both = grads_q[j] + pltpu.roll(dk_acc[j] * SCALE, HP, 1)
            g_ref[pl.ds(at, rows), 0:128] = both.astype(BF16)
            g_ref[pl.ds(at, rows), 128:256] = dv_acc[j].astype(BF16)


def attend_back_kernel(lone_last, me_ref, *refs):
    if not lone_last:
        attend_back_body(2, me_ref, refs)
        return
    last = pl.num_programs(0) - 1

    @pl.when(pl.program_id(0) < last)
    def _():
        attend_back_body(2, me_ref, refs)

    @pl.when(pl.program_id(0) == last)
    def _():
        attend_back_body(1, me_ref, refs)


def slot_of(me, block):
    rel = jnp.bitwise_xor(me, block)
    return jnp.bitwise_or((rel & 1) * 2, rel >> 1)


def block_specs(rows, column):
    return [
        pl.BlockSpec((rows, 128), lambda p, m, j=j: (slot_of(m[0], j), column(p))) for j in range(4)
    ]


def attend(me, proj, rows, heads):
    pairs = -(-heads // 2)
    all_rows = 4 * rows
    last_tile = proj.shape[1] // 128 - 1
    return pl.pallas_call(
        partial(attend_kernel, heads % 2 == 1),
        out_shape=(
            jax.ShapeDtypeStruct((all_rows, pairs * 128), BF16),
            jax.ShapeDtypeStruct((pairs, 4, 8, rows), F32),
        ),
        grid_spec=pltpu.PrefetchScalarGridSpec(
            num_scalar_prefetch=1,
            grid=(pairs,),
            in_specs=[
                s
                for t in range(3)
                for s in block_specs(rows, lambda p, t=t: jnp.minimum(3 * p + t, last_tile))
            ],
            out_specs=[
                pl.BlockSpec((all_rows, 128), lambda p, m: (0, p)),
                pl.BlockSpec((1, 4, 8, rows), lambda p, m: (p, 0, 0, 0)),
            ],
        ),
        cost_estimate=pl.CostEstimate(
            flops=rows, bytes_accessed=rows, transcendentals=0
        ),
    )(me, *([proj] * 12))


def attend_back(me, proj, lse, mixed, grad_mixed, rows, heads):
    pairs = -(-heads // 2)
    all_rows, columns = proj.shape
    last_tile = columns // 128 - 1
    return pl.pallas_call(
        partial(attend_back_kernel, heads % 2 == 1),
        out_shape=jax.ShapeDtypeStruct((all_rows, columns), BF16),
        grid_spec=pltpu.PrefetchScalarGridSpec(
            num_scalar_prefetch=1,
            grid=(pairs,),
            in_specs=[
                s
                for t in range(3)
                for s in block_specs(rows, lambda p, t=t: jnp.minimum(3 * p + t, last_tile))
            ]
            + block_specs(rows, lambda p: p) * 2
            + [pl.BlockSpec((1, 4, 8, rows), lambda p, m: (p, 0, 0, 0))],
            out_specs=pl.BlockSpec((all_rows, 384), lambda p, m: (0, p)),
            scratch_shapes=[pltpu.VMEM((4, rows, 128), F32)] * 2,
        ),
        cost_estimate=pl.CostEstimate(
            flops=rows, bytes_accessed=rows, transcendentals=0
        ),
    )(me, *([proj] * 12), *([grad_mixed] * 4), *([mixed] * 4), lse)


def make(sizes):
    wide, parts = sizes["wide"], sizes["narrow"]

    def on_device(
        tokens, lengths, norm_one, qkv_weight, out_weight, norm_two, up_weight, down_weight, grad_out
    ):
        cell_count, rows, width = tokens.shape
        own_width = qkv_weight.shape[2]
        heads = own_width // HS
        pairs = -(-heads // 2)
        pad_width = pairs * 128
        narrow = Narrow(parts)
        me = lax.axis_index("narrow")
        me_ref = me.reshape(1).astype(jnp.int32)
        length = lengths[0]
        gain_row_one, gain_row_two = norm_one[:, None], norm_two[:, None]
        own_tokens, own_grad = tokens[0].T, grad_out[0].T
        own_live = (me * rows + lax.broadcasted_iota(jnp.int32, (1, rows), 1) < length).astype(F32)

        tok_y, tok_c = narrow.send(own_tokens, 2), narrow.send(own_tokens, 1)

        full = heads // 2
        split = qkv_weight.transpose(0, 2, 1).reshape(3, heads, HS, width)
        split = jnp.pad(split, ((0, 0), (0, 0), (0, HP - HS), (0, 0)))
        pieces = [split[:, : 2 * full].reshape(3, full, 128, width).transpose(1, 0, 2, 3).reshape(full * 384, width)]
        if heads % 2:
            pieces.append(jnp.pad(split[:, 2 * full].reshape(3 * HP, width), ((0, HP), (0, 0))))
        proj = jnp.concatenate(pieces, axis=0)

        def pad_rows(weight):
            split = weight.reshape(heads, HS, width)
            return jnp.pad(split, ((0, 2 * pairs - heads), (0, HP - HS), (0, 0))).reshape(pad_width, width)

        stream = own_tokens.astype(F32)
        normal_one, rstd_one = layer_stats(stream)

        def first_norm(block):
            return (layer_stats(block.astype(F32))[0] * gain_row_one).astype(BF16)

        near = [first_norm(own_tokens), first_norm(tok_c)]
        tok_y = after(tok_y, proj, *near)
        tok_d = narrow.send(tok_y, 1)
        out_y = narrow.send(after(out_weight, tok_y), 2)
        out_c = narrow.send(after(out_weight, tok_y), 1)
        far_norm = [first_norm(tok_y), first_norm(tok_d)]
        rows_one = jnp.concatenate([near[0], far_norm[0], near[1], far_norm[1]], axis=1)
        projected = dot(rows_one, proj, ((0,), (1,))).astype(BF16)
        own_branch = (own_live * own_grad.astype(F32)).astype(BF16)
        own_branch = after(own_branch, tok_y)
        grad_y, grad_c = narrow.send(own_branch, 2), narrow.send(own_branch, 1)
        mixed, lse = attend(me_ref, projected, rows, heads)
        block = lambda a, slot: a[slot * rows : (slot + 1) * rows]
        mixed_y = narrow.send(block(mixed, 1), 2)
        mixed_d = narrow.send(block(mixed, 3), 3)
        mixed_c = narrow.send(block(mixed, 2), 1)
        out_y = after(out_y, mixed)
        out_d = narrow.send(out_y, 1)
        grad_y = after(grad_y, out_y)
        grad_d = narrow.send(grad_y, 1)
        out_all = [pad_rows(after(b, grad_y)) for b in (out_weight, out_y, out_c, out_d)]
        mixed_own = [block(mixed, 0), mixed_y, mixed_c, mixed_d]
        branch = sum(dot(w, m, ((0,), (1,))) for w, m in zip(out_all, mixed_own))
        middle = stream + own_live * branch
        normal_two, rstd_two = layer_stats(middle)
        own_two = (normal_two * gain_row_two).astype(BF16)
        two_y, two_c = narrow.send(own_two, 2), narrow.send(own_two, 1)
        grad_rows = jnp.concatenate([after(own_branch, own_two), grad_y, grad_c, grad_d], axis=1)
        grad_hidden = dot(down_weight, grad_rows, ((1,), (0,)))
        two_y = after(two_y, grad_hidden)
        two_d = narrow.send(two_y, 1)
        rows_two = jnp.concatenate([own_two, two_y, two_c, two_d], axis=1)
        pre_act = dot(up_weight, rows_two, ((0,), (0,)))
        cdf = 0.5 * (1.0 + lax.erf(pre_act * 0.5**0.5))
        slope = cdf + pre_act * jnp.exp(-0.5 * pre_act * pre_act) * (0.5 / jnp.pi) ** 0.5
        hidden = (pre_act * cdf).astype(BF16)
        grad_pre = (grad_hidden * slope).astype(BF16)

        def wide_sum(hops, part):
            return WideSum(wide, hops, part)

        half = 2 * rows
        down = wide_sum((1, 2, 4), dot(hidden, grad_rows, ((1,), (1,))).astype(BF16))
        mark = down.advance()

        grad_pre_on = after(grad_pre, mark)
        sent = dot(up_weight, grad_pre_on[:, half:], ((1,), (0,))).astype(BF16)
        got_two = narrow.send(sent, 1)
        kept_two = dot(up_weight, after(grad_pre_on[:, :half], sent), ((1,), (0,)))
        got_two = after(got_two, kept_two).astype(F32)
        far_sum = (kept_two[:, rows:] + got_two[:, rows:]).astype(BF16)
        far_two = narrow.send(far_sum, 2)
        near_two = kept_two[:, :rows] + got_two[:, :rows]
        up = wide_sum((2, 1, 4), dot(rows_two, after(grad_pre_on, far_sum), ((1,), (1,))).astype(BF16))
        mark = up.advance()
        grad_normed_two = near_two + after(far_two, mark).astype(F32)
        gain_two = jnp.sum(grad_normed_two * normal_two, axis=1)
        grad_middle = own_grad.astype(F32) + layer_back(grad_normed_two * gain_row_two, normal_two, rstd_two)
        grad_attn = (own_live * grad_middle).astype(BF16)
        piece = [dot(grad_attn, w, ((0,), (1,))).astype(BF16) for w in out_all]
        mix_y, mix_d, mix_c = narrow.send(piece[1], 2), narrow.send(piece[3], 3), narrow.send(piece[2], 1)
        hidden_on = after(hidden, *piece)
        mlp_sent = dot(down_weight, hidden_on[:, half:], ((0,), (0,))).astype(BF16)
        mlp_got = narrow.send(mlp_sent, 1)
        mlp_kept = dot(down_weight, after(hidden_on[:, :half], mlp_sent), ((0,), (0,)))
        mix_y = after(mix_y, mlp_kept)
        grad_mixed = jnp.concatenate([piece[0], mix_y, mix_c, mix_d], axis=0)
        mark = down.advance(grad_mixed)
        attn_on = after(grad_attn, mark)
        attn_y, attn_c = narrow.send(attn_on, 2), narrow.send(attn_on, 1)
        grad_proj = attend_back(me_ref, projected, lse, mixed, after(grad_mixed, attn_on), rows, heads)
        mark = up.advance(grad_proj)
        mark = down.advance(mark)
        grad_proj = after(grad_proj, mark)
        attn_y = after(attn_y, grad_proj)
        attn_d = narrow.send(attn_y, 1)
        mlp_got = after(mlp_got, attn_y).astype(F32)
        mlp_far = (mlp_kept[:, rows:] + mlp_got[:, rows:]).astype(BF16)
        mlp_near = mlp_kept[:, :rows] + mlp_got[:, :rows]
        mlp_send_far = narrow.send(after(mlp_far, attn_y), 2)

        found = dot(grad_proj[:, : 3 * heads * HP], rows_one, ((0,), (1,))).astype(BF16)
        fields = [found[: full * 384].reshape(full, 3, 2, HP, width)[:, :, :, :HS]]
        fields[0] = fields[0].transpose(1, 0, 2, 3, 4).reshape(3, full * 2 * HS, width)
        if heads % 2:
            fields.append(found[full * 384 :].reshape(3, HP, width)[:, :HS])
        qkv_part = jnp.concatenate(fields, axis=1).reshape(3 * own_width, width)
        cut = -(-own_width // 16) * 32
        low = 3 * own_width - cut
        filled = lambda a: jnp.pad(a, ((0, cut // 2 - a.shape[0]), (0, 0)))
        first = WideSum(wide, (1, 2, 4), qkv_part[:cut], 3 * own_width)
        mark = first.advance()
        mark = up.advance(mark)
        attn_rows = jnp.concatenate([grad_attn, attn_y, attn_c, after(attn_d, mark)], axis=1)
        out_part = dot(mixed[:, : heads * HP], attn_rows, ((0,), (1,))).astype(BF16)
        out_part = out_part.reshape(heads, HP, width)[:, :HS].reshape(own_width, width)
        second_part = jnp.concatenate([filled(qkv_part[cut:]), filled(out_part)], axis=0)
        second = WideSum(wide, (1, 2, 4), second_part, last=True)
        mark = second.advance()
        mark = first.advance(mark)
        mark = down.advance(mark)
        mark = up.advance(mark)
        mark = second.advance(mark)
        grad_proj = after(grad_proj, mark)
        one_sent = dot(proj, grad_proj[half:], ((0,), (1,))).astype(BF16)
        one_got = narrow.send(one_sent, 1)
        one_kept = dot(proj, after(grad_proj[:half], one_sent), ((0,), (1,)))
        one_got = after(one_got, one_kept).astype(F32)
        one_sum = (one_kept[:, rows:] + one_got[:, rows:]).astype(BF16)
        one_far = narrow.send(one_sum, 2)
        one_near = one_kept[:, :rows] + one_got[:, :rows]
        mark = down.advance(one_sum)
        mark = up.advance(mark)
        mark = first.advance(mark)
        mark = second.advance(mark)
        mlp_own = mlp_near + after(mlp_send_far, mark).astype(F32)
        block_output = (middle + own_live * mlp_own).astype(BF16)
        grad_normed_one = one_near + after(one_far, block_output).astype(F32)
        gain_one = jnp.sum(grad_normed_one * normal_one, axis=1)
        grad_stream = layer_back(grad_normed_one * gain_row_one, normal_one, rstd_one)
        input_grad = (grad_middle + grad_stream).astype(BF16)
        gains = jnp.stack([gain_one, gain_two])
        for hop in (1, 2):
            gains = gains + narrow.send(gains, hop)
        mark = gains
        turns = [[first, second], [down], [first, second]]
        order = (4, 1, 2) + tuple(8 * 2**i for i in range(wide.bit_length() - 4))
        for hop in order:
            got = lax.ppermute(gains, "wide", [(i, i ^ hop) for i in range(wide)])
            for s in turns.pop(0) if turns else ():
                mark = s.advance(mark, gains)
            gains = gains + after(got, mark)
        mark = up.advance(mark, gains)
        for s in (first, second, down, first, up, second):
            mark = s.advance(mark)

        if wide == 8:
            qkv_grad, out_grad = join_last(
                second.at, second.have, second.other, first.whole, second.rows, own_width
            )
        else:
            qkv_grad = jnp.concatenate([first.whole, second.whole[:low]], axis=0)
            out_grad = second.whole[cut // 2 : cut // 2 + own_width]
        qkv_grad = qkv_grad.reshape(3, own_width, width).transpose(0, 2, 1)
        return (
            block_output.T[None],
            input_grad.T[None],
            gains[0],
            qkv_grad,
            out_grad,
            gains[1],
            up.whole,
            down.whole,
        )

    return on_device


def solution(mesh):
    in_specs = (
        P("wide", "narrow", None),
        P("wide"),
        P(),
        P(None, None, "narrow"),
        P("narrow", None),
        P(),
        P(None, "narrow"),
        P("narrow", None),
        P("wide", "narrow", None),
    )
    out_specs = (
        P("wide", "narrow", None),
        P("wide", "narrow", None),
        P(),
        P(None, None, "narrow"),
        P("narrow", None),
        P(),
        P(None, "narrow"),
        P("narrow", None),
    )
    return jax.shard_map(
        make(dict(mesh.shape)), mesh=mesh, in_specs=in_specs, out_specs=out_specs, check_vma=False
    )
```

```python
from functools import partial

import jax
import jax.numpy as jnp
from jax import lax
from jax.experimental import pallas as pl
from jax.experimental.pallas import tpu as pltpu
from jax.sharding import PartitionSpec as P

HS = 56
HP = 64
F32 = jnp.float32
BF16 = jnp.bfloat16


def layer_stats(values):
    mean = jnp.mean(values, axis=0, keepdims=True)
    center = values - mean
    spread = jnp.mean(center * center, axis=0, keepdims=True)
    rstd = lax.rsqrt(spread + 1e-05)
    return center * rstd, rstd


def layer_back(grad_scaled, normal, rstd):
    first = jnp.mean(grad_scaled, axis=0, keepdims=True)
    second = jnp.mean(grad_scaled * normal, axis=0, keepdims=True)
    return rstd * (grad_scaled - first - normal * second)


def dot(a, b, dims):
    return lax.dot_general(a, b, (dims, ((), ())), preferred_element_type=F32)


def after(value, *deps):
    return lax.optimization_barrier((value, *deps))[0]


class Narrow:
    def __init__(self, size):
        self.perm = {k: [(i, i ^ k) for i in range(size)] for k in (1, 2, 3)}

    def send(self, value, k):
        return lax.ppermute(value, "narrow", self.perm[k])


class WideSum:
    def __init__(self, size, hops, part, out_rows=None, last=False):
        self.size, self.hops, self.part, self.rows = size, hops, part, part.shape[0]
        self.out_rows, self.last = out_rows or self.rows, last
        self.step = 0
        index = lax.axis_index("wide")
        bits = [jnp.bitwise_and(index // hop, 1) for hop in hops]
        self.at = jnp.stack(bits).astype(jnp.int32)

    def send(self, value, turn):
        hop = self.hops[turn]
        self.got = lax.ppermute(value, "wide", [(i, i ^ hop) for i in range(self.size)])
        return value

    def advance(self, *deps):
        if self.size != 8:
            if self.step == 0:
                self.whole = lax.psum(self.part.astype(F32), "wide")
            self.step += 1
            return deps[0] if deps else self.part
        got = after(self.got, *deps) if self.step else None
        self.step += 1
        if self.step == 1:
            halves = self.part.reshape(2, self.rows // 2, self.part.shape[1])
            return self.send(lax.dynamic_index_in_dim(halves, 1 - self.at[0], 0, keepdims=False), 0)
        if self.step == 2:
            quarters = self.part.reshape(4, self.rows // 4, self.part.shape[1])
            got = got.reshape(2, self.rows // 4, got.shape[1])
            place = lambda side: lax.dynamic_index_in_dim(
                quarters, 2 * self.at[0] + side, 0, keepdims=False
            ).astype(F32) + lax.dynamic_index_in_dim(got, side, 0, keepdims=False).astype(F32)
            self.keep = place(self.at[1])
            return self.send(place(1 - self.at[1]).astype(BF16), 1)
        if self.step == 3:
            size = eighth_of(self.rows // 4)
            total = self.keep + got.astype(F32)
            first = self.at[2] == 0
            self.keep = jnp.where(first, total[:size], total[-size:])
            return self.send(jnp.where(first, total[-size:], total[:size]).astype(BF16), 2)
        if self.step == 4:
            self.have = (self.keep + got.astype(F32)).astype(BF16)
            return self.send(self.have, 2)
        if self.step == 5:
            self.have = jnp.concatenate([self.have, got], axis=0)
            return self.send(self.have, 1)
        if self.step == 6:
            self.have = jnp.concatenate([self.have, got], axis=0)
            self.send(self.have, 0)
            if not self.last:
                self.whole = join(self.at, self.have, self.rows, self.out_rows, None)
                return self.whole
            return self.have
        if self.last:
            self.other = got
            return got
        self.whole = join(self.at, got, self.rows, self.out_rows, self.whole)
        return self.whole

    @property
    def done(self):
        return self.step == 7


def eighth_of(quarter):
    return -(-quarter // 16) * 8


def join_kernel(rows, at_ref, half_ref, *refs):
    o_ref = refs[-1]
    eighth = half_ref.shape[0] // 2
    first = at_ref[2] == 0

    @pl.when(first)
    def _():
        o_ref[0:eighth, :] = half_ref[0:eighth, :].astype(F32)
        o_ref[rows - eighth : rows, :] = half_ref[eighth : 2 * eighth, :].astype(F32)

    @pl.when(jnp.logical_not(first))
    def _():
        o_ref[0:eighth, :] = half_ref[eighth : 2 * eighth, :].astype(F32)
        o_ref[rows - eighth : rows, :] = half_ref[0:eighth, :].astype(F32)


def join(at, half, rows, out_rows, whole):
    columns, quarter = half.shape[1], rows // 4
    place = (lambda a: a[0]) if whole is None else (lambda a: 1 - a[0])
    return pl.pallas_call(
        partial(join_kernel, quarter),
        out_shape=jax.ShapeDtypeStruct((out_rows, columns), F32),
        grid_spec=pltpu.PrefetchScalarGridSpec(
            num_scalar_prefetch=1,
            grid=(2,),
            in_specs=[
                pl.BlockSpec((half.shape[0] // 2, columns), lambda i, a: (jnp.bitwise_xor(i, a[1]), 0))
            ]
            + ([] if whole is None else [pl.BlockSpec(memory_space=pl.ANY)]),
            out_specs=pl.BlockSpec((quarter, columns), lambda i, a: (2 * place(a) + i, 0)),
        ),
        input_output_aliases={} if whole is None else {2: 0},
        cost_estimate=pl.CostEstimate(flops=0, bytes_accessed=rows, transcendentals=0),
    )(at, half, *([] if whole is None else [whole]))


def join_last_kernel(rows, at_ref, own_ref, other_ref, whole_ref, o_whole_ref, o_rest_ref):
    eighth = own_ref.shape[0] // 2
    step = pl.program_id(0)
    for mine, half_ref in ((True, own_ref), (False, other_ref)):
        for tail, o_ref in ((0, o_whole_ref), (1, o_rest_ref)):
            for bit in (0, 1):
                here = (step // 2 == tail) & ((at_ref[0] == tail) == mine) & (at_ref[2] == bit)

                @pl.when(here)
                def _(half_ref=half_ref, o_ref=o_ref, bit=bit):
                    low, high = (0, eighth) if bit == 0 else (eighth, 0)
                    o_ref[0:eighth, :] = half_ref[low : low + eighth, :].astype(F32)
                    o_ref[rows - eighth : rows, :] = half_ref[high : high + eighth, :].astype(F32)


def join_last(at, own, other, whole, rows, rest_rows):
    columns, quarter = own.shape[1], rows // 4
    half = pl.BlockSpec((own.shape[0] // 2, columns), lambda i, a: (jnp.bitwise_xor(i & 1, a[1]), 0))
    return pl.pallas_call(
        partial(join_last_kernel, quarter),
        out_shape=[
            jax.ShapeDtypeStruct(whole.shape, F32),
            jax.ShapeDtypeStruct((rest_rows, columns), F32),
        ],
        grid_spec=pltpu.PrefetchScalarGridSpec(
            num_scalar_prefetch=1,
            grid=(4,),
            in_specs=[half, half, pl.BlockSpec(memory_space=pl.ANY)],
            out_specs=[
                pl.BlockSpec((quarter, columns), lambda i, a: (4 + jnp.minimum(i, 1), 0)),
                pl.BlockSpec((quarter, columns), lambda i, a: (jnp.maximum(i - 2, 0), 0)),
            ],
        ),
        input_output_aliases={3: 0},
        cost_estimate=pl.CostEstimate(flops=0, bytes_accessed=rows, transcendentals=0),
    )(at, own, other, whole)


LOG2E = 1.4426950408889634
SCALE = HS**-0.5


def nt(a, b):
    return lax.dot_general(a, b, (((1,), (1,)), ((), ())), preferred_element_type=F32)


def nn(a, b):
    return lax.dot_general(a, b, (((1,), (0,)), ((), ())), preferred_element_type=F32)


def half_of(values, which):
    lane = lax.broadcasted_iota(jnp.int32, values.shape, 1)
    keep = lane < HP if which == 0 else lane >= HP
    return jnp.where(keep, values, jnp.zeros_like(values))


def causal_tile(rows):
    key = lax.broadcasted_iota(jnp.int32, (rows, rows), 0)
    query = lax.broadcasted_iota(jnp.int32, (rows, rows), 1)
    return key <= query


def swap_halves(values):
    return pltpu.roll(values.astype(F32), HP, 1).astype(BF16)


def pair_operands(first, second, third, heads):
    if heads == 2:
        return first, second, third
    lone = half_of(second, 0)
    return half_of(first, 0), half_of(swap_halves(first), 0), lone


def attend_kernel(lone_last, me_ref, *refs):
    first, second, third, (o_ref, lse_ref) = refs[0:4], refs[4:8], refs[8:12], refs[12:14]
    me = me_ref[0]
    rows = first[0].shape[0]

    def body(heads):
        tiles = [pair_operands(first[j][...], second[j][...], third[j][...], heads) for j in range(4)]
        value_t = [tiles[j][2].T for j in range(4)]
        causal = causal_tile(rows)
        for a in range(4):
            outs = []
            for h in range(heads):
                query = half_of(tiles[a][0], h)
                score = [nt(tiles[j][1], query) for j in range(a + 1)]
                score[a] = jnp.where(causal, score[a], -1e30)
                top = jnp.max(score[0], axis=0, keepdims=True)
                for j in range(1, a + 1):
                    top = jnp.maximum(top, jnp.max(score[j], axis=0, keepdims=True))
                top = top * (SCALE * LOG2E)
                total = jnp.zeros((1, rows), F32)
                acc = jnp.zeros((HP, rows), F32)
                for j in range(a + 1):
                    p = jnp.exp2(score[j] * (SCALE * LOG2E) - top)
                    total = total + jnp.sum(p, axis=0, keepdims=True)
                    acc = acc + nn(value_t[j][h * HP : (h + 1) * HP], p.astype(BF16))
                outs.append(acc / total)
                lse_ref[0, a, h : h + 1, :] = top + jnp.log2(total)
            if heads == 1:
                outs.append(jnp.zeros((HP, rows), F32))
            at = pl.multiple_of(slot_of(me, a) * rows, rows)
            o_ref[pl.ds(at, rows), :] = jnp.concatenate(outs, axis=0).T.astype(BF16)

    if not lone_last:
        body(2)
        return
    last = pl.num_programs(0) - 1

    @pl.when(pl.program_id(0) < last)
    def _():
        body(2)

    @pl.when(pl.program_id(0) == last)
    def _():
        body(1)


def attend_back_body(heads, me_ref, refs):
    first, second, third, do, o = (refs[4 * i : 4 * i + 4] for i in range(5))
    lse_ref, g_ref, dk_acc, dv_acc = refs[20:24]
    me = me_ref[0]
    rows = first[0].shape[0]
    tiles = [pair_operands(first[j][...], second[j][...], third[j][...], heads) for j in range(4)]
    key_t = [tiles[j][1].T for j in range(4)]
    causal = causal_tile(rows)
    grads_q = []
    for a in range(4):
        grad = do[a][...]
        product = (grad.astype(F32) * o[a][...].astype(F32)).T
        parts = []
        for h in range(heads):
            query, grad_h = half_of(tiles[a][0], h), half_of(grad, h)
            inner = jnp.sum(product[h * HP : (h + 1) * HP], axis=0, keepdims=True)
            lse = lse_ref[0, a, h : h + 1, :]
            dq = jnp.zeros((HP, rows), F32)
            for j in range(a + 1):
                score = nt(tiles[j][1], query) * (SCALE * LOG2E) - lse
                if j == a:
                    score = jnp.where(causal, score, -1e30)
                p = jnp.exp2(score)
                ds = (p * (nt(tiles[j][2], grad_h) - inner)).astype(BF16)
                dv, dk = nn(p.astype(BF16), grad_h), nn(ds, query)
                if a == j and h == 0:
                    dv_acc[j], dk_acc[j] = dv, dk
                else:
                    dv_acc[j] = dv_acc[j] + dv
                    dk_acc[j] = dk_acc[j] + dk
                dq = dq + nn(key_t[j][h * HP : (h + 1) * HP], ds)
            parts.append(dq * SCALE)
        if heads == 1:
            parts.append(jnp.zeros((HP, rows), F32))
        grads_q.append(jnp.concatenate(parts, axis=0).T)
    for j in range(4):
        at = pl.multiple_of(slot_of(me, j) * rows, rows)
        if heads == 2:
            g_ref[pl.ds(at, rows), 0:128] = grads_q[j].astype(BF16)
            g_ref[pl.ds(at, rows), 128:256] = (dk_acc[j] * SCALE).astype(BF16)
            g_ref[pl.ds(at, rows), 256:384] = dv_acc[j].astype(BF16)
        else:
            both = grads_q[j] + pltpu.roll(dk_acc[j] * SCALE, HP, 1)
            g_ref[pl.ds(at, rows), 0:128] = both.astype(BF16)
            g_ref[pl.ds(at, rows), 128:256] = dv_acc[j].astype(BF16)


def attend_back_kernel(lone_last, me_ref, *refs):
    if not lone_last:
        attend_back_body(2, me_ref, refs)
        return
    last = pl.num_programs(0) - 1

    @pl.when(pl.program_id(0) < last)
    def _():
        attend_back_body(2, me_ref, refs)

    @pl.when(pl.program_id(0) == last)
    def _():
        attend_back_body(1, me_ref, refs)


def slot_of(me, block):
    rel = jnp.bitwise_xor(me, block)
    return jnp.bitwise_or((rel & 1) * 2, rel >> 1)


def block_specs(rows, column):
    return [
        pl.BlockSpec((rows, 128), lambda p, m, j=j: (slot_of(m[0], j), column(p))) for j in range(4)
    ]


def attend(me, proj, rows, heads):
    pairs = -(-heads // 2)
    all_rows = 4 * rows
    last_tile = proj.shape[1] // 128 - 1
    return pl.pallas_call(
        partial(attend_kernel, heads % 2 == 1),
        out_shape=(
            jax.ShapeDtypeStruct((all_rows, pairs * 128), BF16),
            jax.ShapeDtypeStruct((pairs, 4, 8, rows), F32),
        ),
        grid_spec=pltpu.PrefetchScalarGridSpec(
            num_scalar_prefetch=1,
            grid=(pairs,),
            in_specs=[
                s
                for t in range(3)
                for s in block_specs(rows, lambda p, t=t: jnp.minimum(3 * p + t, last_tile))
            ],
            out_specs=[
                pl.BlockSpec((all_rows, 128), lambda p, m: (0, p)),
                pl.BlockSpec((1, 4, 8, rows), lambda p, m: (p, 0, 0, 0)),
            ],
        ),
        cost_estimate=pl.CostEstimate(
            flops=rows, bytes_accessed=rows, transcendentals=0
        ),
    )(me, *([proj] * 12))


def attend_back(me, proj, lse, mixed, grad_mixed, rows, heads):
    pairs = -(-heads // 2)
    all_rows, columns = proj.shape
    last_tile = columns // 128 - 1
    return pl.pallas_call(
        partial(attend_back_kernel, heads % 2 == 1),
        out_shape=jax.ShapeDtypeStruct((all_rows, columns), BF16),
        grid_spec=pltpu.PrefetchScalarGridSpec(
            num_scalar_prefetch=1,
            grid=(pairs,),
            in_specs=[
                s
                for t in range(3)
                for s in block_specs(rows, lambda p, t=t: jnp.minimum(3 * p + t, last_tile))
            ]
            + block_specs(rows, lambda p: p) * 2
            + [pl.BlockSpec((1, 4, 8, rows), lambda p, m: (p, 0, 0, 0))],
            out_specs=pl.BlockSpec((all_rows, 384), lambda p, m: (0, p)),
            scratch_shapes=[pltpu.VMEM((4, rows, 128), F32)] * 2,
        ),
        cost_estimate=pl.CostEstimate(
            flops=rows, bytes_accessed=rows, transcendentals=0
        ),
    )(me, *([proj] * 12), *([grad_mixed] * 4), *([mixed] * 4), lse)


def make(sizes):
    wide, parts = sizes["wide"], sizes["narrow"]

    def on_device(
        tokens, lengths, norm_one, qkv_weight, out_weight, norm_two, up_weight, down_weight, grad_out
    ):
        cell_count, rows, width = tokens.shape
        own_width = qkv_weight.shape[2]
        heads = own_width // HS
        pairs = -(-heads // 2)
        pad_width = pairs * 128
        narrow = Narrow(parts)
        me = lax.axis_index("narrow")
        me_ref = me.reshape(1).astype(jnp.int32)
        length = lengths[0]
        gain_row_one, gain_row_two = norm_one[:, None], norm_two[:, None]
        own_tokens, own_grad = tokens[0].T, grad_out[0].T
        own_live = (me * rows + lax.broadcasted_iota(jnp.int32, (1, rows), 1) < length).astype(F32)

        tok_y, tok_c = narrow.send(own_tokens, 2), narrow.send(own_tokens, 1)

        full = heads // 2
        split = qkv_weight.transpose(0, 2, 1).reshape(3, heads, HS, width)
        split = jnp.pad(split, ((0, 0), (0, 0), (0, HP - HS), (0, 0)))
        pieces = [split[:, : 2 * full].reshape(3, full, 128, width).transpose(1, 0, 2, 3).reshape(full * 384, width)]
        if heads % 2:
            pieces.append(jnp.pad(split[:, 2 * full].reshape(3 * HP, width), ((0, HP), (0, 0))))
        proj = jnp.concatenate(pieces, axis=0)

        def pad_rows(weight):
            split = weight.reshape(heads, HS, width)
            return jnp.pad(split, ((0, 2 * pairs - heads), (0, HP - HS), (0, 0))).reshape(pad_width, width)

        stream = own_tokens.astype(F32)
        normal_one, rstd_one = layer_stats(stream)

        def first_norm(block):
            return (layer_stats(block.astype(F32))[0] * gain_row_one).astype(BF16)

        near = [first_norm(own_tokens), first_norm(tok_c)]
        tok_y = after(tok_y, proj, *near)
        tok_d = narrow.send(tok_y, 1)
        out_y = narrow.send(after(out_weight, tok_y), 2)
        out_c = narrow.send(after(out_weight, tok_y), 1)
        far_norm = [first_norm(tok_y), first_norm(tok_d)]
        rows_one = jnp.concatenate([near[0], far_norm[0], near[1], far_norm[1]], axis=1)
        projected = dot(rows_one, proj, ((0,), (1,))).astype(BF16)
        own_branch = (own_live * own_grad.astype(F32)).astype(BF16)
        own_branch = after(own_branch, tok_y)
        grad_y, grad_c = narrow.send(own_branch, 2), narrow.send(own_branch, 1)
        mixed, lse = attend(me_ref, projected, rows, heads)
        block = lambda a, slot: a[slot * rows : (slot + 1) * rows]
        mixed_y = narrow.send(block(mixed, 1), 2)
        mixed_d = narrow.send(block(mixed, 3), 3)
        mixed_c = narrow.send(block(mixed, 2), 1)
        out_y = after(out_y, mixed)
        out_d = narrow.send(out_y, 1)
        grad_y = after(grad_y, out_y)
        grad_d = narrow.send(grad_y, 1)
        out_all = [pad_rows(after(b, grad_y)) for b in (out_weight, out_y, out_c, out_d)]
        mixed_own = [block(mixed, 0), mixed_y, mixed_c, mixed_d]
        branch = sum(dot(w, m, ((0,), (1,))) for w, m in zip(out_all, mixed_own))
        middle = stream + own_live * branch
        normal_two, rstd_two = layer_stats(middle)
        own_two = (normal_two * gain_row_two).astype(BF16)
        two_y, two_c = narrow.send(own_two, 2), narrow.send(own_two, 1)
        grad_rows = jnp.concatenate([after(own_branch, own_two), grad_y, grad_c, grad_d], axis=1)
        grad_hidden = dot(down_weight, grad_rows, ((1,), (0,)))
        two_y = after(two_y, grad_hidden)
        two_d = narrow.send(two_y, 1)
        rows_two = jnp.concatenate([own_two, two_y, two_c, two_d], axis=1)
        pre_act = dot(up_weight, rows_two, ((0,), (0,)))
        cdf = 0.5 * (1.0 + lax.erf(pre_act * 0.5**0.5))
        slope = cdf + pre_act * jnp.exp(-0.5 * pre_act * pre_act) * (0.5 / jnp.pi) ** 0.5
        hidden = (pre_act * cdf).astype(BF16)
        grad_pre = (grad_hidden * slope).astype(BF16)

        def wide_sum(hops, part):
            return WideSum(wide, hops, part)

        half = 2 * rows
        down = wide_sum((1, 2, 4), dot(hidden, grad_rows, ((1,), (1,))).astype(BF16))
        mark = down.advance()

        grad_pre_on = after(grad_pre, mark)
        sent = dot(up_weight, grad_pre_on[:, half:], ((1,), (0,))).astype(BF16)
        got_two = narrow.send(sent, 1)
        kept_two = dot(up_weight, after(grad_pre_on[:, :half], sent), ((1,), (0,)))
        got_two = after(got_two, kept_two).astype(F32)
        far_sum = (kept_two[:, rows:] + got_two[:, rows:]).astype(BF16)
        far_two = narrow.send(far_sum, 2)
        near_two = kept_two[:, :rows] + got_two[:, :rows]
        up = wide_sum((2, 1, 4), dot(rows_two, after(grad_pre_on, far_sum), ((1,), (1,))).astype(BF16))
        mark = up.advance()
        grad_normed_two = near_two + after(far_two, mark).astype(F32)
        gain_two = jnp.sum(grad_normed_two * normal_two, axis=1)
        grad_middle = own_grad.astype(F32) + layer_back(grad_normed_two * gain_row_two, normal_two, rstd_two)
        grad_attn = (own_live * grad_middle).astype(BF16)
        piece = [dot(grad_attn, w, ((0,), (1,))).astype(BF16) for w in out_all]
        mix_y, mix_d, mix_c = narrow.send(piece[1], 2), narrow.send(piece[3], 3), narrow.send(piece[2], 1)
        hidden_on = after(hidden, *piece)
        mlp_sent = dot(down_weight, hidden_on[:, half:], ((0,), (0,))).astype(BF16)
        mlp_got = narrow.send(mlp_sent, 1)
        mlp_kept = dot(down_weight, after(hidden_on[:, :half], mlp_sent), ((0,), (0,)))
        mix_y = after(mix_y, mlp_kept)
        grad_mixed = jnp.concatenate([piece[0], mix_y, mix_c, mix_d], axis=0)
        mark = down.advance(grad_mixed)
        attn_on = after(grad_attn, mark)
        attn_y, attn_c = narrow.send(attn_on, 2), narrow.send(attn_on, 1)
        grad_proj = attend_back(me_ref, projected, lse, mixed, after(grad_mixed, attn_on), rows, heads)
        mark = up.advance(grad_proj)
        mark = down.advance(mark)
        grad_proj = after(grad_proj, mark)
        attn_y = after(attn_y, grad_proj)
        attn_d = narrow.send(attn_y, 1)
        mlp_got = after(mlp_got, attn_y).astype(F32)
        mlp_far = (mlp_kept[:, rows:] + mlp_got[:, rows:]).astype(BF16)
        mlp_near = mlp_kept[:, :rows] + mlp_got[:, :rows]
        mlp_send_far = narrow.send(after(mlp_far, attn_y), 2)

        found = dot(grad_proj[:, : 3 * heads * HP], rows_one, ((0,), (1,))).astype(BF16)
        fields = [found[: full * 384].reshape(full, 3, 2, HP, width)[:, :, :, :HS]]
        fields[0] = fields[0].transpose(1, 0, 2, 3, 4).reshape(3, full * 2 * HS, width)
        if heads % 2:
            fields.append(found[full * 384 :].reshape(3, HP, width)[:, :HS])
        qkv_part = jnp.concatenate(fields, axis=1).reshape(3 * own_width, width)
        cut = -(-own_width // 16) * 32
        low = 3 * own_width - cut
        filled = lambda a: jnp.pad(a, ((0, cut // 2 - a.shape[0]), (0, 0)))
        first = WideSum(wide, (1, 2, 4), qkv_part[:cut], 3 * own_width)
        mark = first.advance()
        mark = up.advance(mark)
        attn_rows = jnp.concatenate([grad_attn, attn_y, attn_c, after(attn_d, mark)], axis=1)
        out_part = dot(mixed[:, : heads * HP], attn_rows, ((0,), (1,))).astype(BF16)
        out_part = out_part.reshape(heads, HP, width)[:, :HS].reshape(own_width, width)
        second_part = jnp.concatenate([filled(qkv_part[cut:]), filled(out_part)], axis=0)
        second = WideSum(wide, (1, 2, 4), second_part, last=True)
        mark = second.advance()
        mark = first.advance(mark)
        mark = down.advance(mark)
        mark = up.advance(mark)
        mark = second.advance(mark)
        grad_proj = after(grad_proj, mark)
        one_sent = dot(proj, grad_proj[half:], ((0,), (1,))).astype(BF16)
        one_got = narrow.send(one_sent, 1)
        one_kept = dot(proj, after(grad_proj[:half], one_sent), ((0,), (1,)))
        one_got = after(one_got, one_kept).astype(F32)
        one_sum = (one_kept[:, rows:] + one_got[:, rows:]).astype(BF16)
        one_far = narrow.send(one_sum, 2)
        one_near = one_kept[:, :rows] + one_got[:, :rows]
        mark = down.advance(one_sum)
        mark = first.advance(mark)
        mark = up.advance(mark)
        mark = second.advance(mark)
        mlp_own = mlp_near + after(mlp_send_far, mark).astype(F32)
        block_output = (middle + own_live * mlp_own).astype(BF16)
        grad_normed_one = one_near + after(one_far, block_output).astype(F32)
        gain_one = jnp.sum(grad_normed_one * normal_one, axis=1)
        grad_stream = layer_back(grad_normed_one * gain_row_one, normal_one, rstd_one)
        input_grad = (grad_middle + grad_stream).astype(BF16)
        gains = jnp.stack([gain_one, gain_two])
        for hop in (1, 2):
            gains = gains + narrow.send(gains, hop)
        mark = gains
        turns = [[first, second], [down], [first, second]]
        order = (4, 1, 2) + tuple(8 * 2**i for i in range(wide.bit_length() - 4))
        for hop in order:
            got = lax.ppermute(gains, "wide", [(i, i ^ hop) for i in range(wide)])
            for s in turns.pop(0) if turns else ():
                mark = s.advance(mark, gains)
            gains = gains + after(got, mark)
        mark = up.advance(mark, gains)
        for s in (first, second, down, first, up, second):
            mark = s.advance(mark)

        if wide == 8:
            qkv_grad, out_grad = join_last(
                second.at, second.have, second.other, first.whole, second.rows, own_width
            )
        else:
            qkv_grad = jnp.concatenate([first.whole, second.whole[:low]], axis=0)
            out_grad = second.whole[cut // 2 : cut // 2 + own_width]
        qkv_grad = qkv_grad.reshape(3, own_width, width).transpose(0, 2, 1)
        return (
            block_output.T[None],
            input_grad.T[None],
            gains[0],
            qkv_grad,
            out_grad,
            gains[1],
            up.whole,
            down.whole,
        )

    return on_device


def solution(mesh):
    in_specs = (
        P("wide", "narrow", None),
        P("wide"),
        P(),
        P(None, None, "narrow"),
        P("narrow", None),
        P(),
        P(None, "narrow"),
        P("narrow", None),
        P("wide", "narrow", None),
    )
    out_specs = (
        P("wide", "narrow", None),
        P("wide", "narrow", None),
        P(),
        P(None, None, "narrow"),
        P("narrow", None),
        P(),
        P(None, "narrow"),
        P("narrow", None),
    )
    return jax.shard_map(
        make(dict(mesh.shape)), mesh=mesh, in_specs=in_specs, out_specs=out_specs, check_vma=False
    )
```
